32 devices in a mesh: cuts: 1, mode: 32 (over z, y, x, core).
Axes of the slice: x: 2, y: 2, z: 4, core: 2. Of those that a mesh axis runs over, the one named last changes fastest.
Arguments:
- branch_in: bfloat16 [4, 2, 2048, 1024], P(None, None, ('cuts', 'mode')), may hold values from -6 to 6
- column_order: int32 [4, 1024], replicated, may hold values from 0 to 1023, each once within a row
- gate_a: bfloat16 [2, 1024, 1024], P(None, 'mode'), may hold values from -0.125 to 0.125
- gate_b: bfloat16 [2, 1024, 1024], P(None, 'mode'), may hold values from -0.125 to 0.125
Outputs:
- joined: bfloat16 [2, 512, 2, 128], P(None, ('cuts', 'mode'))
The draws below stay inside these ranges and needn't reach their ends.
Inputs may be any that keep to these rules, and one draw needn't show every extreme that they name: Each row of column_order names every column state once.
All inputs are finite; a program needn't handle non-finite values.
Results may differ from the reference program's by a relative error of at most 0.014.
Values may be sent and summed in bfloat16 or wider, within the bound.
A program may use at most 128 MiB of HBM per device.

```python
import jax
import jax.numpy as jnp

C = 1024
SHARED = 4096
RD = 64
KEPT = 4
CYCLES = 2
ROWS = 2048
GROUP = 32
JOIN = 128
N_MODE = 32


def level_of(rng, dims, cuts, smallest, high):
    factor_of = 1.0
    for position, shards_of in cuts:
        draws = jax.random.uniform(jax.random.fold_in(jax.random.fold_in(rng, 6), position), (shards_of,), jnp.float32, smallest / len(cuts), high / len(cuts))
        factor_of = factor_of * jnp.repeat(jnp.exp(draws), dims[position] // shards_of).reshape((-1,) + (1,) * (len(dims) - 1 - position))
    return factor_of


def normal_values(own_key, shape, scale, most, cuts=(), dtype=jnp.bfloat16):
    result = scale * jax.random.normal(own_key, shape, jnp.float32)
    if cuts:
        result = result * level_of(own_key, shape, cuts, -0.22, 0.18)
    return jnp.clip(result, -most, most).astype(dtype)


def setup_inputs(seed: int = 0, part: int = 0) -> dict:
    key_list = jax.random.split(jax.random.key(seed), 5)
    part_keys = jax.random.split(jax.random.fold_in(key_list[4], part), 5)
    return {
        "branch_in": normal_values(part_keys[0], (4, 2, ROWS, C), 1.0, 6.0, ((2, 32),)),
        "column_order": jax.vmap(lambda own: jax.random.permutation(own, C))(jax.random.split(key_list[1], 4)).reshape((4, C)).astype(jnp.int32),
        "gate_a": normal_values(key_list[2], (2, C, C), (2 * C) ** -0.5, 0.125, ((1, 32),)),
        "gate_b": normal_values(key_list[3], (2, C, C), (2 * C) ** -0.5, 0.125, ((1, 32),)),
    }


def complex_product(pair_tensor, layer_block):
    real_part = jnp.dot(pair_tensor[0], layer_block[0], preferred_element_type=jnp.float32) - jnp.dot(pair_tensor[1], layer_block[1], preferred_element_type=jnp.float32)
    imag_part = jnp.dot(pair_tensor[0], layer_block[1], preferred_element_type=jnp.float32) + jnp.dot(pair_tensor[1], layer_block[0], preferred_element_type=jnp.float32)
    return jnp.stack([real_part, imag_part]).astype(jnp.bfloat16)


def regroup(pair_tensor):
    pieces = pair_tensor.reshape(2, N_MODE, RD, N_MODE, GROUP)
    return jnp.transpose(pieces, (0, 3, 2, 1, 4)).reshape(2, ROWS, C)


def reference(branch_in, column_order, gate_a, gate_b):
    join_scale = (2.0 * SHARED) ** -0.5
    finals = []
    for branch in range(4):
        state = jnp.take(branch_in[branch], column_order[branch].astype(jnp.int32), axis=2)
        for layer_number in range(2 * CYCLES):
            if layer_number > 0:
                state = regroup(state)
            layer_block = gate_a if layer_number % 2 == 0 else gate_b
            state = complex_product(state, layer_block)
        finals.append(state)
    results = []
    for pair_number in range(2):
        left_part = finals[2 * pair_number].reshape(2, KEPT, JOIN, SHARED)
        right_part = finals[2 * pair_number + 1].reshape(2, SHARED, KEPT, JOIN)
        blocks = []
        for batch in range(KEPT):
            left_real = left_part[0, batch]
            left_imag = left_part[1, batch]
            right_real = right_part[0, :, batch, :]
            right_imag = right_part[1, :, batch, :]
            real_part = jnp.dot(left_real, right_real, preferred_element_type=jnp.float32) - jnp.dot(left_imag, right_imag, preferred_element_type=jnp.float32)
            imag_part = jnp.dot(left_real, right_imag, preferred_element_type=jnp.float32) + jnp.dot(left_imag, right_real, preferred_element_type=jnp.float32)
            blocks.append(jnp.stack([real_part, imag_part], axis=1))
        stacked = jnp.concatenate(blocks, axis=0)
        results.append((stacked * join_scale).astype(jnp.bfloat16))
    return jnp.stack(results)
```

```python
import jax
import jax.numpy as jnp
from jax import lax
from jax.experimental import pallas as pl
from jax.experimental.pallas import tpu as pltpu
from jax.sharding import PartitionSpec as P

SHARED = 4096
KEPT = 4
CYCLES = 2
F32 = jnp.float32
BF16 = jnp.bfloat16


def complex_dot(left_real, left_imag, right_real, right_imag):
    real_part = jnp.dot(left_real, right_real, preferred_element_type=F32) - jnp.dot(
        left_imag, right_imag, preferred_element_type=F32
    )
    imag_part = jnp.dot(left_real, right_imag, preferred_element_type=F32) + jnp.dot(
        left_imag, right_real, preferred_element_type=F32
    )
    return real_part, imag_part


def layers_plain(state, orders, whole_a, whole_b):
    parts, devices, sides, share, width = state.shape
    group = width // devices
    iota = lax.broadcasted_iota(jnp.int32, (width, width), 0)
    halves = []
    for side in range(sides):
        one_hot = (iota == orders[side][None, :]).astype(BF16)
        piece = state[:, :, side].reshape(parts * devices * share, width)
        halves.append(
            jnp.dot(piece, one_hot, preferred_element_type=F32)
            .astype(BF16)
            .reshape(parts, devices, share, width)
        )
    state = jnp.stack(halves, axis=2)
    for layer in range(2 * CYCLES):
        if layer > 0:
            pieces = state.reshape(parts, devices, sides, share, devices, group)
            state = pieces.transpose(0, 4, 2, 3, 1, 5)
        flat = state.reshape(parts, devices * sides * share, width)
        gate = whole_a if layer % 2 == 0 else whole_b
        state = jnp.stack(complex_dot(flat[0], flat[1], gate[0], gate[1])).astype(BF16)
    return state.reshape(parts, devices, sides, share, width)


LANES = 128
HIGH = 8


def swap_lane_blocks(blocks, group):
    count = len(blocks)
    lane = lax.broadcasted_iota(jnp.int32, (HIGH, LANES), 1) // group
    bit = count // 2
    while bit:
        low = (lane // bit) % 2 == 0
        new = list(blocks)
        for i in range(count):
            if i & bit == 0:
                first, second = blocks[i], blocks[i | bit]
                new[i] = jnp.where(low, first, pltpu.roll(second, bit * group, 1))
                new[i | bit] = jnp.where(low, pltpu.roll(first, LANES - bit * group, 1), second)
        blocks = new
        bit //= 2
    return blocks


def whole_kernel(
    devices,
    branch,
    orders,
    gate_a,
    gate_b,
    out,
    gates,
    raw,
    dealt,
    landed,
    state,
    other,
    final,
    product,
    hot,
    comb,
    left_out,
    left_in,
    right,
    part_out,
    part_in,
    own_sem,
    relay,
    deal_send,
    deal_recv,
    gate_send,
    gate_recv,
    line_send,
    line_recv,
    left_send,
    left_recv,
    right_send,
    right_recv,
    part_send,
    part_recv,
):
    me = lax.axis_index("mode")
    width = hot.shape[1]
    rows = product.shape[0]
    half = width // 2
    groups = width // devices
    packed = LANES // groups
    share = HIGH // 2
    in_pair = devices // 2
    chips = in_pair // 2
    quarter = SHARED // width
    z, y, x, c = (me // 8, me // 4 % 2, me // 2 % 2, me % 2)
    pair = me // in_pair
    slot = me % in_pair
    first = me - slot
    depth_z = devices // 8
    every = slice(None)
    shards = (gate_a, gate_b)

    load = pltpu.make_async_copy(branch, raw, own_sem.at[4])
    load.start()
    own = [
        pltpu.make_async_copy(shards[g], gates.at[g, :, z, y, x, c], own_sem.at[g])
        for g in range(2)
    ]
    for copy in own:
        copy.start()

    barrier = pltpu.get_barrier_semaphore()
    for bit in (1, 2, 4):
        pl.semaphore_signal(barrier, inc=1, device_id={"mode": me ^ bit})

    @pl.when(z > 0)
    def _():
        pl.semaphore_signal(barrier, inc=1, device_id={"mode": me - 8})

    @pl.when(z < depth_z - 1)
    def _():
        pl.semaphore_signal(barrier, inc=1, device_id={"mode": me + 8})

    def remote(src, dst, ssem, rsem, target):
        return pltpu.make_async_remote_copy(
            src_ref=src,
            dst_ref=dst,
            send_sem=ssem,
            recv_sem=rsem,
            device_id={"mode": target},
            device_id_type=pl.DeviceIdType.MESH,
        )

    swaps = (
        {
            "p0": (0, y, x, 4),
            "p1": (1, y, x, 2),
            "q0": (0, every, x, 2),
            "q1": (1, y, every, 4),
            "c0": (every, y, x, 1),
            "d0": (0, 1 - y, x, 1),
            "d1": (1, y, 1 - x, 1),
            "e0": (0, every, 1 - x, 1),
            "e1": (1, 1 - y, every, 1),
        },
        {
            "q0": (0, every, x, 2),
            "q1": (1, y, every, 4),
            "d0": (0, every, x, 1),
            "d1": (1, y, every, 1),
            "e0": (0, every, 1 - x, 1),
            "e1": (1, 1 - y, every, 1),
            "p0": (0, y, x, 4),
            "p1": (1, y, x, 2),
        },
    )

    def swap_copy(g, name, place):
        part, at_y, at_x, bit = swaps[g][name]
        k = list(swaps[g]).index(name)
        here = gates.at[g, part, z + place, at_y, at_x, c]
        first = name in ("p0", "p1", "c0") and place == 0
        src = (shards[g] if name == "c0" else shards[g].at[part]) if first else here
        n = place + depth_z - 1
        return remote(src, here, gate_send.at[g, k, n], gate_recv.at[g, k, n], me ^ bit)

    def on_round(r, action):
        for place in (0,) if r == 0 else (-r, r):
            if place == 0:
                action(place)
            else:

                @pl.when((z + place >= 0) & (z + place < depth_z))
                def _():
                    action(place)

    def send(g, r, *which):
        def action(place):
            for name in which:
                swap_copy(g, name, place).start()

        on_round(r, action)

    def pass_on(g, r, got, which):
        def action(place):
            for name in got:
                swap_copy(g, name, place).wait_recv()
            for name in which:
                swap_copy(g, name, place).start()

        on_round(r, action)

    def swaps_end(g, recv, *which):
        for r in range(depth_z):

            def action(place):
                for name in which:
                    copy = swap_copy(g, name, place)
                    if recv is True:
                        copy.wait_recv()
                    else:
                        copy.wait_send()

            on_round(r, action)

    threads = ((0, every, y, x), (1, 0, every, x), (1, 1, y, every))

    def line_copy(t, up, k):
        g, part, at_y, at_x = threads[t]
        block = z - k if up else z + k
        here = gates.at[g, part, block, at_y, at_x, c]
        src = shards[0] if t == 0 and k == 0 else here
        n = (t * 2 + up) * (depth_z - 1) + k
        return remote(
            src, here, line_send.at[n], line_recv.at[n], me + 8 if up else me - 8
        )

    def line_sends(up, k):
        return (z >= k) & (z < depth_z - 1) if up else (z + k < depth_z) & (z > 0)

    def line_gets(up, k):
        return z >= k + 1 if up else z + 1 + k < depth_z

    def line_start(k, *which):
        for up in (1, 0):

            @pl.when(line_sends(up, k))
            def _():
                for t in which:
                    line_copy(t, up, k).start()

    def line_arrive(k, *which):
        for up in (1, 0):

            @pl.when(line_gets(up, k))
            def _():
                for t in which:
                    g, part, at_y, at_x = threads[t]
                    block = z - 1 - k if up else z + 1 + k
                    here = gates.at[g, part, block, at_y, at_x, c]
                    n = (t * 2 + up) * (depth_z - 1) + k
                    remote(
                        here, here, line_send.at[n], line_recv.at[n], me ^ 8
                    ).wait_recv()

    def line_end():
        for t in range(len(threads)):
            for up in (1, 0):
                for k in range(depth_z - 1):

                    @pl.when(line_sends(up, k))
                    def _():
                        line_copy(t, up, k).wait_send()


    def deal_copy(side, o):
        return remote(
            dealt.at[side, me ^ o],
            landed.at[side, me],
            deal_send.at[side, o],
            deal_recv.at[side, o],
            me ^ o,
        )

    def start_deal(side, low, high):
        @pl.loop(low, high)
        def _(o):
            deal_copy(side, o).start()

    def wait_deal(side):
        @pl.loop(1, devices)
        def _(o):
            remote(
                dealt.at[side, me],
                landed.at[side, me ^ o],
                deal_send.at[side, o],
                deal_recv.at[side, o],
                me ^ o,
            ).wait_recv()

    def make_deal(side):
        o = lax.broadcasted_iota(jnp.int32, (rows, rows), 0)
        i = lax.broadcasted_iota(jnp.int32, (rows, rows), 1)
        to, part, own_row = o // HIGH % in_pair, o // share % 2, o % share
        if side == 0:
            q = to % KEPT * in_pair + own_row * quarter + to // KEPT
        else:
            q = to * share + own_row
        source = o // (rows // 2) * (rows // 2) + part * (rows // 4) + q
        pick = jnp.where(i == source, 1.0, 0.0).astype(BF16)
        lines = raw.shape[2]
        for n in range(2):
            block = jnp.concatenate(
                [
                    raw[2 * p + side, part, :, n * half : (n + 1) * half]
                    for p in range(2)
                    for part in range(2)
                ],
                axis=0,
            )
            moved = jnp.dot(pick, block, preferred_element_type=F32)
            product[:, n * half : (n + 1) * half] = moved
        both = [
            product[:, n * half : (n + 1) * half].reshape(devices, HIGH, half) for n in range(2)
        ]
        dealt[side] = jnp.concatenate(both, axis=1).astype(BF16)

    def make_hot(side, k):
        order = orders[pl.ds(2 * pair + side, 1), :]
        span = width // 4
        source = lax.broadcasted_iota(jnp.int32, (span, width), 0) + k * span
        hot[side, pl.ds(k * span, span)] = jnp.where(source == order, 1.0, 0.0).astype(BF16)

    def make_comb(k):
        new = lax.broadcasted_iota(jnp.int32, (1, width), 1)
        natural = (
            new // share % 8 * LANES
            + new // LANES * 16
            + new // 32 % 2 * 8
            + new % share * 2
            + new // 64 % 2
        )
        span = width // 4
        source = lax.broadcasted_iota(jnp.int32, (span, width), 0) + k * span
        comb[pl.ds(k * span, span)] = jnp.where(source == natural, 1.0, 0.0).astype(BF16)

    def relay_signal(k, target):
        pl.semaphore_signal(relay.at[k], inc=1, device_id={"mode": target})

    upper = lax.broadcasted_iota(jnp.int32, (HIGH, LANES), 0) < share
    sign = jnp.where(upper, -1.0, 1.0)

    def turned(block):
        return sign * pltpu.roll(block, share, 0)

    def put(to, at, n, block):
        to[at, n * LANES : (n + 1) * LANES] = block.astype(BF16)
        lines = block.shape[0] // HIGH
        to[at, width + n * LANES : width + (n + 1) * LANES] = jnp.concatenate(
            [turned(block[i * HIGH : (i + 1) * HIGH]) for i in range(lines)], axis=0
        ).astype(BF16)

    span = packed * HIGH
    tile = 2 * LANES
    tiles = [slice(n * tile, (n + 1) * tile) for n in range(width // tile)]

    def take_in(side, to):
        landed[side, pl.ds(me, 1)] = dealt[side, pl.ds(me, 1)]
        wide = landed[side].astype(F32)
        for n in range(2):
            final[:, n * half : (n + 1) * half] = (
                wide[:, n * HIGH : (n + 1) * HIGH].reshape(rows, half).astype(BF16)
            )
        for n, cols in enumerate(tiles):
            moved = jnp.dot(final[...], hot[side, :, cols], preferred_element_type=F32)
            for i in range(rows // span):
                at = slice(i * span, (i + 1) * span)
                for u in range(2):
                    put(to, at, 2 * n + u, moved[at, u * LANES : (u + 1) * LANES])

    def multiplied(g, source, cols):
        block = gates[g, :, :, :, :, :, :, cols].reshape(2 * width, tile)
        return jnp.dot(source[...], block, preferred_element_type=F32)

    def layer(g, source, to):
        for n, cols in enumerate(tiles):
            value = multiplied(g, source, cols)
            for a in range(rows // span):
                for u in range(2):
                    blocks = [
                        value[
                            a * span + i * HIGH : a * span + (i + 1) * HIGH,
                            u * LANES : (u + 1) * LANES,
                        ]
                        for i in range(packed)
                    ]
                    blocks = swap_lane_blocks(blocks, groups)
                    s = 2 * n + u
                    put(to, slice(s * span, (s + 1) * span), a, jnp.concatenate(blocks, axis=0))

    def left_ready(g, source):
        for cols in tiles:
            final[:, cols] = multiplied(g, source, cols).astype(BF16)
        for n, cols in enumerate(tiles):
            moved = jnp.dot(final[...], comb[:, cols], preferred_element_type=F32).astype(BF16)
            for core in range(2):
                for u in range(2):
                    left_out[core, n * 2 + u] = moved[
                        core * (rows // 2) : (core + 1) * (rows // 2), u * LANES : (u + 1) * LANES
                    ]

    def left_copy(o):
        to = slot ^ o
        return remote(
            left_out.at[to % 2, to // 2], left_in.at[slot], left_send.at[o], left_recv.at[o], me ^ o
        )

    def left_wait(o):
        return remote(
            left_out.at[0, 0], left_in.at[slot ^ o], left_send.at[o], left_recv.at[o], me ^ o
        )

    own_left = pltpu.make_async_copy(left_out.at[c, slot // 2], left_in.at[slot], own_sem.at[2])

    def right_ready(g, source):
        for n, cols in enumerate(tiles):
            value = multiplied(g, source, cols)
            for u in range(2):
                e, batch = (2 * n + u) // KEPT, (2 * n + u) % KEPT
                place = jnp.where(batch // 2 == c, c, 2)
                for r in range(devices // 4):
                    lines = [
                        value[
                            (r * 4 + i) * HIGH : (r * 4 + i + 1) * HIGH,
                            u * LANES : (u + 1) * LANES,
                        ]
                        for i in range(4)
                    ]
                    parts = ([], [])
                    for i in range(0, 4, 2):
                        low, top = lines[i], lines[i + 1]
                        parts[0].append(jnp.where(upper, low, pltpu.roll(top, share, 0)))
                        parts[1].append(jnp.where(upper, pltpu.roll(low, share, 0), top))
                    for part in range(2):
                        right[place, part, e, batch % 2, r * 16 : (r + 1) * 16] = jnp.concatenate(
                            parts[part], axis=0
                        ).astype(BF16)

    right_copy = remote(right.at[2], right.at[c], right_send.at[0], right_recv.at[0], me ^ 1)

    def join():
        for g in range(2):
            at = slice(g * (rows // 4), (g + 1) * (rows // 4))
            lefts = jnp.concatenate(
                [
                    jnp.concatenate([left_in[j * KEPT + h, at] for j in range(quarter)], axis=1)
                    for h in range(KEPT)
                ],
                axis=0,
            )
            step = devices
            rights = jnp.concatenate(
                [
                    jnp.concatenate(
                        [right[core, part, e, g, j * step : (j + 1) * step] for part in range(2)],
                        axis=1,
                    )
                    for j in range(quarter)
                    for e in range(2)
                    for core in range(2)
                ],
                axis=0,
            )
            both = jnp.dot(lefts, rights, preferred_element_type=F32)
            span = rows // KEPT
            for a in range(HIGH):
                lines = []
                for h in range(0, KEPT, 2):
                    low = both[h * span + a * HIGH : h * span + (a + 1) * HIGH]
                    top = both[(h + 1) * span + a * HIGH : (h + 1) * span + (a + 1) * HIGH]
                    a0, b0, a1, b1 = (low[:, :LANES], low[:, LANES:], top[:, :LANES], top[:, LANES:])
                    real = jnp.where(
                        upper, a0 - pltpu.roll(b0, share, 0), pltpu.roll(a1, share, 0) - b1
                    )
                    imag = jnp.where(
                        upper, b0 + pltpu.roll(a0, share, 0), pltpu.roll(b1, share, 0) + a1
                    )
                    lines.append(jnp.concatenate([real, imag], axis=1))
                part_out[g * HIGH + a] = jnp.concatenate(lines, axis=0).astype(BF16)

    from_chip = me // 2

    def part_copy(i):
        return remote(
            part_out.at[i],
            part_in.at[from_chip],
            part_send.at[i],
            part_recv.at[from_chip],
            c * in_pair + i,
        )

    own_part = pltpu.make_async_copy(part_out.at[slot], part_in.at[from_chip], own_sem.at[3])

    through = ("q0", "q1", "d0", "d1")
    start = ("p0", "p1", "c0")

    def first_a(r):
        line_arrive(r - 1, 0)
        if r < depth_z - 1:
            line_start(r, 0)
        send(0, r, *start)

    def second_a(r):
        pass_on(0, r, ("p0", "p1"), through)

    def third(g, r):
        pass_on(g, r, ("q0", "q1"), ("e0", "e1"))

    def first_b(r):
        line_arrive(r - 1, 1, 2)
        if r < depth_z - 1:
            line_start(r, 1, 2)
        send(1, r, *through)

    def finish_phase_a():
        swaps_end(0, False, *swaps[0])
        swaps_end(1, False, *list(swaps[1])[:6])
        for name in ("p0", "p1"):
            swap_copy(1, name, 0).wait_send()
        line_end()

        @pl.loop(1, devices)
        def _(o):
            for side in range(2):
                deal_copy(side, o).wait_send()

    inner = ((z > 0) & (z < depth_z - 1)).astype(jnp.int32)
    pl.semaphore_wait(barrier, 4 + inner)

    line_start(0, 0)
    send(1, 0, "p0", "p1")
    send(0, 0, *start)
    relay_signal(0, me ^ 2)
    load.wait()
    make_deal(0)
    pl.semaphore_wait(relay.at[0], 1)
    relay_signal(1, me ^ 4)
    for copy in own:
        copy.wait()
    pass_on(1, 0, ("p0", "p1"), ())
    line_start(0, 1, 2)
    pl.semaphore_wait(relay.at[1], 1)

    @pl.when(z > 0)
    def _():
        pl.semaphore_wait(relay.at[2], 1)

    @pl.when(z < depth_z - 1)
    def _():
        relay_signal(2, me + 8)

    first_a(1)
    second_a(0)
    send(1, 0, *through)

    @pl.when(z < depth_z - 1)
    def _():
        pl.semaphore_wait(relay.at[3], 1)

    @pl.when(z > 0)
    def _():
        relay_signal(3, me - 8)

    start_deal(0, 1, devices)
    first_a(2)
    first_b(1)
    second_a(1)
    make_deal(1)
    first_a(3)
    third(0, 0)
    second_a(2)
    first_b(2)
    start_deal(1, 1, devices)
    third(1, 0)
    third(0, 1)
    second_a(3)
    first_b(3)
    third(1, 1)
    third(0, 2)
    for k in range(4):
        make_hot(0, k)
    third(0, 3)
    third(1, 2)
    for k in range(4):
        make_hot(1, k)
        make_comb(k)
    third(1, 3)
    wait_deal(0)
    take_in(0, state)
    swaps_end(0, True, "c0", "d0", "d1", "e0", "e1")
    layer(0, state, other)
    swaps_end(1, True, "d0", "d1", "e0", "e1")
    layer(1, other, state)
    layer(0, state, other)
    left_ready(1, other)

    @pl.loop(1, in_pair)
    def _(o):
        left_copy(o).start()

    own_left.start()
    wait_deal(1)
    take_in(1, state)
    layer(0, state, other)
    layer(1, other, state)
    layer(0, state, other)
    right_ready(1, other)
    right_copy.start()
    own_left.wait()

    @pl.loop(1, in_pair)
    def _(o):
        left_wait(o).wait_recv()

    right_copy.wait()
    join()

    @pl.loop(0, in_pair)
    def _(i):
        target = c * in_pair + i

        @pl.when(target != me)
        def _():
            part_copy(i).start()

        @pl.when(target == me)
        def _():
            own_part.start()

    @pl.loop(0, in_pair)
    def _(i):
        @pl.when((me // in_pair == c) & (i == from_chip))
        def _():
            own_part.wait()

        @pl.when((me // in_pair != c) | (i != from_chip))
        def _():
            remote(
                part_out.at[0], part_in.at[i], part_send.at[0], part_recv.at[i], me ^ 1
            ).wait_recv()

    scale = (2.0 * SHARED) ** (-0.5)
    for p in range(2):
        total = part_in[p * chips].astype(F32)
        for i in range(1, chips):
            total += part_in[p * chips + i].astype(F32)
        out[p] = (total * scale).astype(BF16)

    @pl.loop(0, in_pair)
    def _(i):
        @pl.when(c * in_pair + i != me)
        def _():
            part_copy(i).wait_send()

    @pl.loop(1, in_pair)
    def _(o):
        left_copy(o).wait_send()

    finish_phase_a()


def run_whole(branch, orders, gate_a, gate_b, devices):
    width = branch.shape[3]
    depth = gate_a.shape[1]
    rows = devices * HIGH
    lines = 2 * HIGH
    in_pair = devices // 2
    dma = pltpu.SemaphoreType.DMA
    vmem = pl.BlockSpec(memory_space=pltpu.VMEM)
    hbm = pl.BlockSpec(memory_space=pl.ANY)
    return pl.pallas_call(
        lambda *refs: whole_kernel(devices, *refs),
        out_shape=jax.ShapeDtypeStruct((2, lines, 2 * LANES), BF16),
        in_specs=[hbm, vmem, hbm, hbm],
        out_specs=vmem,
        scratch_shapes=[
            pltpu.VMEM((2, 2, devices // 8, 2, 2, 2, depth, width), BF16),
            pltpu.VMEM(branch.shape, BF16),
            pltpu.VMEM((2, devices, lines, width // 2), BF16),
            pltpu.VMEM((2, devices, lines, width // 2), BF16),
            pltpu.VMEM((rows, 2 * width), BF16),
            pltpu.VMEM((rows, 2 * width), BF16),
            pltpu.VMEM((rows, width), BF16),
            pltpu.VMEM((rows, width), F32),
            pltpu.VMEM((2, width, width), BF16),
            pltpu.VMEM((width, width), BF16),
            pltpu.VMEM((2, in_pair // 2, rows // 2, LANES), BF16),
            pltpu.VMEM((in_pair, rows // 2, LANES), BF16),
            pltpu.VMEM((3, 2, 2, 2, rows // 2, LANES), BF16),
            pltpu.VMEM((in_pair, lines, 2 * LANES), BF16),
            pltpu.VMEM((in_pair, lines, 2 * LANES), BF16),
            dma((5,)),
            pltpu.SemaphoreType.REGULAR((4,)),
            dma((2, devices)),
            dma((2, devices)),
            dma((2, 9, 2 * (devices // 8) - 1)),
            dma((2, 9, 2 * (devices // 8) - 1)),
            dma((6 * (devices // 8 - 1),)),
            dma((6 * (devices // 8 - 1),)),
            dma((in_pair,)),
            dma((in_pair,)),
            dma((1,)),
            dma((1,)),
            dma((in_pair,)),
            dma((in_pair,)),
        ],
        compiler_params=pltpu.CompilerParams(
            collective_id=0, has_side_effects=True, vmem_limit_bytes=60 * 2**20
        ),
    )(branch, orders, gate_a, gate_b)


def local(branch_in, column_order, gate_a, gate_b):
    join_scale = (2.0 * SHARED) ** (-0.5)
    devices = lax.axis_size("mode")
    me = lax.axis_index("mode")
    branches, parts, rows, width = branch_in.shape
    quarter = SHARED // width
    holders = devices // (2 * quarter)
    share = rows // (quarter * holders)
    pair = me // (quarter * holders)
    lines = 2 * parts * share
    if lines == 2 * HIGH and holders == KEPT and devices == HIGH * KEPT == width // devices:
        done = run_whole(branch_in, column_order, gate_a, gate_b, devices)
        return done.reshape(2, lines, 2, LANES)
    dealt = branch_in.reshape(2, 2, parts, holders, share, quarter, width)
    dealt = dealt.transpose(0, 5, 3, 2, 1, 4, 6).reshape(devices, parts, 2, share, width)
    orders = lax.dynamic_slice_in_dim(column_order, 2 * pair, 2, 0)
    whole_a = lax.all_gather(gate_a, "mode", axis=1, tiled=True)
    whole_b = lax.all_gather(gate_b, "mode", axis=1, tiled=True)
    dealt = lax.all_to_all(dealt, "mode", split_axis=0, concat_axis=0, tiled=True)
    state = dealt.transpose(1, 0, 2, 3, 4)
    state = layers_plain(state, orders, whole_a, whole_b)

    split = holders // KEPT
    piece = width // split
    free = devices * rows * width // (SHARED * KEPT)
    own_group = [
        [start * holders + h for h in range(holders)] for start in range(2 * quarter)
    ]
    pair_group = [
        [start * quarter * holders + d for d in range(quarter * holders)] for start in range(2)
    ]
    left = state[:, :, 0].reshape(parts, KEPT, devices // KEPT, share, split, piece)
    left = left.transpose(1, 4, 0, 2, 3, 5).reshape(
        holders, parts, devices // KEPT, share, piece
    )
    left = lax.all_to_all(
        left, "mode", split_axis=0, concat_axis=0, tiled=True, axis_index_groups=own_group
    )
    left = left.transpose(1, 2, 0, 3, 4).reshape(parts, free, piece)
    right = state[:, :, 1].reshape(parts, quarter, split, devices // (quarter * split), share, width)
    line = rows * width
    step = KEPT * free
    if width % step == 0:
        several = width // step
        right = right.reshape(
            parts, quarter, split, devices // (quarter * split), share, several, KEPT, free
        )
        right = right.transpose(1, 6, 2, 0, 3, 4, 5, 7)
        right = right.reshape(
            quarter * KEPT * split, parts, devices // (quarter * split), share, several, free
        )
        right = lax.all_to_all(
            right, "mode", split_axis=0, concat_axis=0, tiled=True, axis_index_groups=pair_group
        )
        right = right.reshape(
            quarter, holders, parts, devices // (quarter * split), share, several, free
        )
        right = right.transpose(2, 3, 1, 4, 0, 5, 6).reshape(parts, piece, free)
    else:
        spans = step // width
        kept_row = KEPT // spans
        right = right.reshape(
            parts, quarter, split, devices // (quarter * split), share, kept_row, free
        )
        own_j = me // holders % quarter
        g_high = own_j % spans
        slots = jnp.zeros(
            (quarter, spans, kept_row, split, parts, devices // (quarter * split), share, free), BF16
        )
        filled = right.transpose(1, 5, 2, 0, 3, 4, 6)
        slots = lax.dynamic_update_slice_in_dim(slots, filled[:, None], g_high, 1)
        slots = slots.reshape(
            quarter * KEPT * split, parts, devices // (quarter * split), share, free
        )
        slots = lax.all_to_all(
            slots, "mode", split_axis=0, concat_axis=0, tiled=True, axis_index_groups=pair_group
        )
        slots = slots.reshape(
            quarter // spans, spans, holders, parts, devices // (quarter * split), share, free
        )
        my_g = me % holders // split
        slots = lax.dynamic_index_in_dim(slots, my_g // kept_row, 1, keepdims=False)
        right = slots.transpose(2, 3, 1, 4, 0, 5).reshape(parts, piece, free)
    real_part, imag_part = complex_dot(left[0], left[1], right[0], right[1])
    partial = jnp.stack([real_part, imag_part], axis=1)
    return finish(partial, join_scale, devices, quarter, split)


def finish(partial, join_scale, devices, quarter, split):
    me = lax.axis_index("mode")
    free = partial.shape[0]
    holders = devices // (2 * quarter)
    sum_group = [
        [((p * quarter + j) * KEPT + g) * split + w for j in range(quarter) for w in range(split)]
        for p in range(2)
        for g in range(KEPT)
    ]
    count = quarter * split
    chunks = partial.astype(BF16).reshape(count, free // count, 2, free)
    chunks = lax.all_to_all(
        chunks, "mode", split_axis=0, concat_axis=0, tiled=True, axis_index_groups=sum_group
    )
    done = (jnp.sum(chunks.astype(F32), axis=0) * join_scale).astype(BF16)
    halves = done.reshape(2, free // (2 * count), 2, free)
    pair = me // (quarter * holders)
    same = lax.dynamic_index_in_dim(halves, pair, 0, keepdims=False)
    other = lax.dynamic_index_in_dim(halves, 1 - pair, 0, keepdims=False)
    same_pairs, other_pairs = [], []
    for d in range(devices):
        p, j, g, w = (
            d // (quarter * holders),
            d // holders % quarter,
            d // split % KEPT,
            d % split,
        )
        base = g * (devices // KEPT) + 2 * (j * split + w)
        same_pairs.append((d, base + p))
        other_pairs.append((d, base + 1 - p))
    from_same = lax.ppermute(same, "mode", same_pairs)
    from_other = lax.ppermute(other, "mode", other_pairs)
    parity = me % 2
    first = jnp.where(parity == 0, from_same, from_other)
    second = jnp.where(parity == 0, from_other, from_same)
    return jnp.stack([first, second])


def solution(mesh):
    in_specs = (
        P(None, None, ("cuts", "mode"), None),
        P(),
        P(None, "mode", None),
        P(None, "mode", None),
    )
    out_specs = P(None, ("cuts", "mode"), None, None)
    return jax.shard_map(local, mesh=mesh, in_specs=in_specs, out_specs=out_specs, check_vma=False)
```

```python
import jax
import jax.numpy as jnp
from jax import lax
from jax.experimental import pallas as pl
from jax.experimental.pallas import tpu as pltpu
from jax.sharding import PartitionSpec as P

SHARED = 4096
KEPT = 4
CYCLES = 2
F32 = jnp.float32
BF16 = jnp.bfloat16


def complex_dot(left_real, left_imag, right_real, right_imag):
    real_part = jnp.dot(left_real, right_real, preferred_element_type=F32) - jnp.dot(
        left_imag, right_imag, preferred_element_type=F32
    )
    imag_part = jnp.dot(left_real, right_imag, preferred_element_type=F32) + jnp.dot(
        left_imag, right_real, preferred_element_type=F32
    )
    return real_part, imag_part


def layers_plain(state, orders, whole_a, whole_b):
    parts, devices, sides, share, width = state.shape
    group = width // devices
    iota = lax.broadcasted_iota(jnp.int32, (width, width), 0)
    halves = []
    for side in range(sides):
        one_hot = (iota == orders[side][None, :]).astype(BF16)
        piece = state[:, :, side].reshape(parts * devices * share, width)
        halves.append(
            jnp.dot(piece, one_hot, preferred_element_type=F32)
            .astype(BF16)
            .reshape(parts, devices, share, width)
        )
    state = jnp.stack(halves, axis=2)
    for layer in range(2 * CYCLES):
        if layer > 0:
            pieces = state.reshape(parts, devices, sides, share, devices, group)
            state = pieces.transpose(0, 4, 2, 3, 1, 5)
        flat = state.reshape(parts, devices * sides * share, width)
        gate = whole_a if layer % 2 == 0 else whole_b
        state = jnp.stack(complex_dot(flat[0], flat[1], gate[0], gate[1])).astype(BF16)
    return state.reshape(parts, devices, sides, share, width)


LANES = 128
HIGH = 8


def swap_lane_blocks(blocks, group):
    count = len(blocks)
    lane = lax.broadcasted_iota(jnp.int32, (HIGH, LANES), 1) // group
    bit = count // 2
    while bit:
        low = (lane // bit) % 2 == 0
        new = list(blocks)
        for i in range(count):
            if i & bit == 0:
                first, second = blocks[i], blocks[i | bit]
                new[i] = jnp.where(low, first, pltpu.roll(second, bit * group, 1))
                new[i | bit] = jnp.where(low, pltpu.roll(first, LANES - bit * group, 1), second)
        blocks = new
        bit //= 2
    return blocks


def whole_kernel(
    devices,
    branch,
    order_in,
    gate_a,
    gate_b,
    out,
    gates,
    raw,
    dealt,
    landed,
    state,
    other,
    final,
    product,
    hot,
    comb,
    left_out,
    left_in,
    right,
    part_out,
    part_in,
    orders,
    own_sem,
    relay,
    deal_send,
    deal_recv,
    gate_send,
    gate_recv,
    line_send,
    line_recv,
    left_send,
    left_recv,
    right_send,
    right_recv,
    part_send,
    part_recv,
):
    me = lax.axis_index("mode")
    width = hot.shape[1]
    rows = product.shape[0]
    half = width // 2
    groups = width // devices
    packed = LANES // groups
    share = HIGH // 2
    in_pair = devices // 2
    chips = in_pair // 2
    quarter = SHARED // width
    z, y, x, c = (me // 8, me // 4 % 2, me // 2 % 2, me % 2)
    pair = me // in_pair
    slot = me % in_pair
    first = me - slot
    depth_z = devices // 8
    depth = gates.shape[6]
    every = slice(None)
    shards = (gate_a, gate_b)

    load = pltpu.make_async_copy(branch, raw, own_sem.at[4])
    load.start()
    load_orders = pltpu.make_async_copy(order_in, orders, own_sem.at[3])
    load_orders.start()
    own = [
        pltpu.make_async_copy(shards[g], gates.at[g, :, z, y, x, c], own_sem.at[g])
        for g in range(2)
    ]
    for copy in own:
        copy.start()

    barrier = pltpu.get_barrier_semaphore()
    far = tuple(8 * k for k in range(1, depth_z))
    greeted = tuple(range(1, 8)) + far
    for o in greeted:
        pl.semaphore_signal(barrier, inc=1, device_id={"mode": me ^ o})

    def remote(src, dst, ssem, rsem, target):
        return pltpu.make_async_remote_copy(
            src_ref=src,
            dst_ref=dst,
            send_sem=ssem,
            recv_sem=rsem,
            device_id={"mode": target},
            device_id_type=pl.DeviceIdType.MESH,
        )

    swaps = (
        {
            "p0": (0, y, x, 4),
            "p1": (1, y, x, 2),
            "q0": (0, every, x, 2),
            "q1": (1, y, every, 4),
            "c0": (every, y, x, 1),
            "d0": (0, 1 - y, x, 1),
            "d1": (1, y, 1 - x, 1),
            "e0": (0, every, 1 - x, 1),
            "e1": (1, 1 - y, every, 1),
        },
        {
            "q0": (0, every, x, 2),
            "q1": (1, y, every, 4),
            "d0": (0, every, x, 1),
            "d1": (1, y, every, 1),
            "e0": (0, every, 1 - x, 1),
            "e1": (1, 1 - y, every, 1),
            "p0": (0, y, x, 4),
            "p1": (1, y, x, 2),
        },
    )

    def swap_copy(g, name, place):
        part, at_y, at_x, bit = swaps[g][name]
        here = gates.at[g, part, z + place, at_y, at_x, c]
        first = name in ("p0", "p1", "c0") and place == 0
        src = (shards[g] if name == "c0" else shards[g].at[part]) if first else here
        n = {"p": z + place, "q": depth_z + z + place}.get(name[0], 2 * depth_z)
        return remote(src, here, gate_send.at[g], gate_recv.at[g, n], me ^ bit)

    def on_round(r, action):
        for place in (0,) if r == 0 else (-r, r):
            if place == 0:
                action(place)
            else:

                @pl.when((z + place >= 0) & (z + place < depth_z))
                def _():
                    action(place)

    def send(g, r, *which):
        def action(place):
            for name in which:
                swap_copy(g, name, place).start()

        on_round(r, action)

    def pass_on(g, r, got, which):
        def action(place):
            plane = gates.at[g, :, z + place]
            if got == "p":
                landing(plane.at[:, y, x, c], gate_recv.at[g, z + place])
            else:
                landing(plane.at[:, :, x, c], gate_recv.at[g, depth_z + z + place])
            for name in which:
                swap_copy(g, name, place).start()

        on_round(r, action)

    def landing(ref, sem):
        pltpu.make_async_copy(ref, ref, sem).wait()

    def from_core_end(g):
        landing(gates.at[g, :, :, :, :, 1 - c], gate_recv.at[g, 2 * depth_z])

    def sent(blocks, sem):
        landing(hot.at[:, : blocks * depth // 2], sem)

    threads = ((0, every, y, x), (1, 0, every, x), (1, 1, y, every))

    def line_copy(t, up, k):
        g, part, at_y, at_x = threads[t]
        block = z - k if up else z + k
        here = gates.at[g, part, block, at_y, at_x, c]
        src = shards[0] if t == 0 and k == 0 else here
        return remote(
            src, here, line_send.at[0], line_recv.at[g, block], me + 8 if up else me - 8
        )

    def line_sends(up, k):
        return (z >= k) & (z < depth_z - 1) if up else (z + k < depth_z) & (z > 0)

    def line_gets(up, k):
        return z >= k + 1 if up else z + 1 + k < depth_z

    def line_start(k, *which):
        for up in (1, 0):

            @pl.when(line_sends(up, k))
            def _():
                for t in which:
                    line_copy(t, up, k).start()

    def line_arrive(k, g):
        for up in (1, 0):

            @pl.when(line_gets(up, k))
            def _():
                block = z - 1 - k if up else z + 1 + k
                plane = gates.at[g, :, block]
                landing(
                    plane.at[:, y, x, c] if g == 0 else plane.at[:, :, x, c], line_recv.at[g, block]
                )


    def deal_copy(side, o):
        return remote(
            dealt.at[side, me ^ o],
            landed.at[side, me],
            deal_send.at[side],
            deal_recv.at[side],
            me ^ o,
        )

    def start_deal(side, low, high):
        @pl.loop(low, high)
        def _(o):
            deal_copy(side, o).start()

    def wait_deal(side):
        landing(landed.at[side, : devices - 1], deal_recv.at[side])

    def make_deal(side):
        o = lax.broadcasted_iota(jnp.int32, (rows, rows), 0)
        i = lax.broadcasted_iota(jnp.int32, (rows, rows), 1)
        to, part, own_row = o // HIGH % in_pair, o // share % 2, o % share
        if side == 0:
            q = to % KEPT * in_pair + own_row * quarter + to // KEPT
        else:
            q = to * share + own_row
        source = o // (rows // 2) * (rows // 2) + part * (rows // 4) + q
        pick = jnp.where(i == source, 1.0, 0.0).astype(BF16)
        lines = raw.shape[2]
        for n in range(2):
            block = jnp.concatenate(
                [
                    raw[2 * p + side, part, :, n * half : (n + 1) * half]
                    for p in range(2)
                    for part in range(2)
                ],
                axis=0,
            )
            moved = jnp.dot(pick, block, preferred_element_type=F32)
            product[:, n * half : (n + 1) * half] = moved
        both = [
            product[:, n * half : (n + 1) * half].reshape(devices, HIGH, half) for n in range(2)
        ]
        dealt[side] = jnp.concatenate(both, axis=1).astype(BF16)

    def make_hot(side, k):
        order = orders[pl.ds(2 * pair + side, 1), :]
        span = width // 4
        source = lax.broadcasted_iota(jnp.int32, (span, width), 0) + k * span
        hot[side, pl.ds(k * span, span)] = jnp.where(source == order, 1.0, 0.0).astype(BF16)

    def make_comb(k):
        new = lax.broadcasted_iota(jnp.int32, (1, width), 1)
        natural = (
            new // share % 8 * LANES
            + new // LANES * 16
            + new // 32 % 2 * 8
            + new % share * 2
            + new // 64 % 2
        )
        span = width // 4
        source = lax.broadcasted_iota(jnp.int32, (span, width), 0) + k * span
        comb[pl.ds(k * span, span)] = jnp.where(source == natural, 1.0, 0.0).astype(BF16)

    def relay_signal(k, target):
        pl.semaphore_signal(relay.at[k], inc=1, device_id={"mode": target})

    upper = lax.broadcasted_iota(jnp.int32, (HIGH, LANES), 0) < share
    sign = jnp.where(upper, -1.0, 1.0)

    def turned(block):
        return sign * pltpu.roll(block, share, 0)

    def put(to, at, n, block):
        to[at, n * LANES : (n + 1) * LANES] = block.astype(BF16)
        lines = block.shape[0] // HIGH
        to[at, width + n * LANES : width + (n + 1) * LANES] = jnp.concatenate(
            [turned(block[i * HIGH : (i + 1) * HIGH]) for i in range(lines)], axis=0
        ).astype(BF16)

    span = packed * HIGH
    tile = 2 * LANES
    tiles = [slice(n * tile, (n + 1) * tile) for n in range(width // tile)]

    def take_in(side, to):
        landed[side, pl.ds(me, 1)] = dealt[side, pl.ds(me, 1)]
        wide = landed[side].astype(F32)
        for n in range(2):
            final[:, n * half : (n + 1) * half] = (
                wide[:, n * HIGH : (n + 1) * HIGH].reshape(rows, half).astype(BF16)
            )
        for n, cols in enumerate(tiles):
            moved = jnp.dot(final[...], hot[side, :, cols], preferred_element_type=F32)
            for i in range(rows // span):
                at = slice(i * span, (i + 1) * span)
                for u in range(2):
                    put(to, at, 2 * n + u, moved[at, u * LANES : (u + 1) * LANES])

    def multiplied(g, source, cols):
        block = gates[g, :, :, :, :, :, :, cols].reshape(2 * width, tile)
        return jnp.dot(source[...], block, preferred_element_type=F32)

    def layer(g, source, to):
        for n, cols in enumerate(tiles):
            value = multiplied(g, source, cols)
            for a in range(rows // span):
                for u in range(2):
                    blocks = [
                        value[
                            a * span + i * HIGH : a * span + (i + 1) * HIGH,
                            u * LANES : (u + 1) * LANES,
                        ]
                        for i in range(packed)
                    ]
                    blocks = swap_lane_blocks(blocks, groups)
                    s = 2 * n + u
                    put(to, slice(s * span, (s + 1) * span), a, jnp.concatenate(blocks, axis=0))

    def left_ready(g, source):
        for cols in tiles:
            final[:, cols] = multiplied(g, source, cols).astype(BF16)
        for n, cols in enumerate(tiles):
            moved = jnp.dot(final[...], comb[:, cols], preferred_element_type=F32).astype(BF16)
            for core in range(2):
                for u in range(2):
                    left_out[core, n * 2 + u] = moved[
                        core * (rows // 2) : (core + 1) * (rows // 2), u * LANES : (u + 1) * LANES
                    ]

    def left_copy(o):
        to = slot ^ o
        return remote(
            left_out.at[to % 2, to // 2], left_in.at[slot], left_send.at[0], left_recv.at[0], me ^ o
        )

    own_left = pltpu.make_async_copy(left_out.at[c, slot // 2], left_in.at[slot], own_sem.at[2])

    def right_ready(g, source):
        for n, cols in enumerate(tiles):
            value = multiplied(g, source, cols)
            for u in range(2):
                e, batch = (2 * n + u) // KEPT, (2 * n + u) % KEPT
                place = jnp.where(batch // 2 == c, c, 2)
                for r in range(devices // 4):
                    lines = [
                        value[
                            (r * 4 + i) * HIGH : (r * 4 + i + 1) * HIGH,
                            u * LANES : (u + 1) * LANES,
                        ]
                        for i in range(4)
                    ]
                    parts = ([], [])
                    for i in range(0, 4, 2):
                        low, top = lines[i], lines[i + 1]
                        parts[0].append(jnp.where(upper, low, pltpu.roll(top, share, 0)))
                        parts[1].append(jnp.where(upper, pltpu.roll(low, share, 0), top))
                    for part in range(2):
                        right[place, part, e, batch % 2, r * 16 : (r + 1) * 16] = jnp.concatenate(
                            parts[part], axis=0
                        ).astype(BF16)

    right_copy = remote(right.at[2], right.at[c], right_send.at[0], right_recv.at[0], me ^ 1)

    def join():
        for g in range(2):
            at = slice(g * (rows // 4), (g + 1) * (rows // 4))
            lefts = jnp.concatenate(
                [
                    jnp.concatenate([left_in[j * KEPT + h, at] for j in range(quarter)], axis=1)
                    for h in range(KEPT)
                ],
                axis=0,
            )
            step = devices
            rights = jnp.concatenate(
                [
                    jnp.concatenate(
                        [right[core, part, e, g, j * step : (j + 1) * step] for part in range(2)],
                        axis=1,
                    )
                    for j in range(quarter)
                    for e in range(2)
                    for core in range(2)
                ],
                axis=0,
            )
            both = jnp.dot(lefts, rights, preferred_element_type=F32)
            span = rows // KEPT
            for a in range(HIGH):
                lines = []
                for h in range(0, KEPT, 2):
                    low = both[h * span + a * HIGH : h * span + (a + 1) * HIGH]
                    top = both[(h + 1) * span + a * HIGH : (h + 1) * span + (a + 1) * HIGH]
                    a0, b0, a1, b1 = (low[:, :LANES], low[:, LANES:], top[:, :LANES], top[:, LANES:])
                    real = jnp.where(
                        upper, a0 - pltpu.roll(b0, share, 0), pltpu.roll(a1, share, 0) - b1
                    )
                    imag = jnp.where(
                        upper, b0 + pltpu.roll(a0, share, 0), pltpu.roll(b1, share, 0) + a1
                    )
                    lines.append(jnp.concatenate([real, imag], axis=1))
                part_out[g * HIGH + a] = jnp.concatenate(lines, axis=0).astype(BF16)

    from_chip = me // 2

    def part_copy(i):
        return remote(
            part_out.at[i],
            part_in.at[from_chip],
            part_send.at[0],
            part_recv.at[0],
            c * in_pair + i,
        )

    own_part = pltpu.make_async_copy(part_out.at[slot], part_in.at[from_chip], part_recv.at[0])

    through = ("q0", "q1", "d0", "d1")
    start = ("p0", "p1", "c0")

    def first_a(r):
        line_arrive(r - 1, 0)
        if r < depth_z - 1:
            line_start(r, 0)
        send(0, r, *start)

    def second_a(r):
        pass_on(0, r, "p", through)

    def third(g, r):
        pass_on(g, r, "q", ("e0", "e1"))

    def first_b(r):
        line_arrive(r - 1, 1)
        if r < depth_z - 1:
            line_start(r, 1, 2)
        send(1, r, *through)

    def finish_phase_a():
        each_a, each_b = 14, 12
        sent(each_a * depth_z, gate_send.at[0])
        sent(each_b * depth_z + 2, gate_send.at[1])
        inner = (z > 0) & (z < depth_z - 1)

        @pl.when(inner)
        def _():
            sent(6 * (depth_z + 1), line_send.at[0])

        @pl.when(jnp.logical_not(inner))
        def _():
            sent(6, line_send.at[0])

        for side in range(2):
            landing(dealt.at[side, : devices - 1], deal_send.at[side])

    pl.semaphore_wait(barrier, len(greeted))
    line_start(0, 0)
    send(1, 0, "p0", "p1")
    send(0, 0, *start)
    for k, o in enumerate(far):
        relay_signal(k, me ^ o)
    load.wait()
    make_deal(0)
    make_deal(1)
    own[0].wait()
    own[1].wait()
    pass_on(1, 0, "p", ())
    line_start(0, 1, 2)
    first_a(1)
    second_a(0)
    send(1, 0, *through)
    for k in range(len(far)):
        pl.semaphore_wait(relay.at[k], 1)
    start_deal(0, 1, 32)
    first_a(2)
    first_b(1)
    second_a(1)
    first_a(3)
    third(0, 0)
    second_a(2)
    first_b(2)
    third(1, 0)
    third(0, 1)
    second_a(3)
    first_b(3)
    third(1, 1)
    third(0, 2)
    start_deal(1, 1, 32)
    load_orders.wait()
    for k in range(4):
        make_hot(0, k)
    third(0, 3)
    third(1, 2)
    for k in range(4):
        make_hot(1, k)
        make_comb(k)
    third(1, 3)
    wait_deal(0)
    take_in(0, state)
    from_core_end(0)
    layer(0, state, other)
    from_core_end(1)
    layer(1, other, state)
    layer(0, state, other)
    left_ready(1, other)

    @pl.loop(1, in_pair)
    def _(o):
        left_copy(o).start()

    own_left.start()
    wait_deal(1)
    take_in(1, state)
    layer(0, state, other)
    layer(1, other, state)
    layer(0, state, other)
    right_ready(1, other)
    right_copy.start()
    own_left.wait()

    landing(left_in.at[: in_pair - 1], left_recv.at[0])

    right_copy.wait()
    join()

    @pl.loop(0, in_pair)
    def _(i):
        target = c * in_pair + i

        @pl.when(target != me)
        def _():
            part_copy(i).start()

        @pl.when(target == me)
        def _():
            own_part.start()

    landing(part_in, part_recv.at[0])
    scale = (2.0 * SHARED) ** (-0.5)
    for p in range(2):
        total = part_in[p * chips].astype(F32)
        for i in range(1, chips):
            total += part_in[p * chips + i].astype(F32)
        out[p] = (total * scale).astype(BF16)

    @pl.when(me // in_pair == c)
    def _():
        landing(part_out.at[: in_pair - 1], part_send.at[0])

    @pl.when(me // in_pair != c)
    def _():
        landing(part_out, part_send.at[0])

    landing(left_in.at[: in_pair - 1], left_send.at[0])
    finish_phase_a()


def run_whole(branch, orders, gate_a, gate_b, devices):
    width = branch.shape[3]
    depth = gate_a.shape[1]
    rows = devices * HIGH
    lines = 2 * HIGH
    in_pair = devices // 2
    dma = pltpu.SemaphoreType.DMA
    vmem = pl.BlockSpec(memory_space=pltpu.VMEM)
    hbm = pl.BlockSpec(memory_space=pl.ANY)
    return pl.pallas_call(
        lambda *refs: whole_kernel(devices, *refs),
        out_shape=jax.ShapeDtypeStruct((2, lines, 2 * LANES), BF16),
        in_specs=[hbm] * 4,
        out_specs=vmem,
        scratch_shapes=[
            pltpu.VMEM((2, 2, devices // 8, 2, 2, 2, depth, width), BF16),
            pltpu.VMEM(branch.shape, BF16),
            pltpu.VMEM((2, devices, lines, width // 2), BF16),
            pltpu.VMEM((2, devices, lines, width // 2), BF16),
            pltpu.VMEM((rows, 2 * width), BF16),
            pltpu.VMEM((rows, 2 * width), BF16),
            pltpu.VMEM((rows, width), BF16),
            pltpu.VMEM((rows, width), F32),
            pltpu.VMEM((2, width, width), BF16),
            pltpu.VMEM((width, width), BF16),
            pltpu.VMEM((2, in_pair // 2, rows // 2, LANES), BF16),
            pltpu.VMEM((in_pair, rows // 2, LANES), BF16),
            pltpu.VMEM((3, 2, 2, 2, rows // 2, LANES), BF16),
            pltpu.VMEM((in_pair, lines, 2 * LANES), BF16),
            pltpu.VMEM((in_pair, lines, 2 * LANES), BF16),
            pltpu.VMEM(orders.shape, jnp.int32),
            dma((5,)),
            pltpu.SemaphoreType.REGULAR((devices // 8 - 1,)),
            dma((2,)),
            dma((2,)),
            dma((2,)),
            dma((2, 2 * (devices // 8) + 1)),
            dma((1,)),
            dma((2, devices // 8)),
            dma((1,)),
            dma((1,)),
            dma((1,)),
            dma((1,)),
            dma((1,)),
            dma((1,)),
        ],
        compiler_params=pltpu.CompilerParams(
            collective_id=0, has_side_effects=True, vmem_limit_bytes=60 * 2**20
        ),
    )(branch, orders, gate_a, gate_b)


def local(branch_in, column_order, gate_a, gate_b):
    join_scale = (2.0 * SHARED) ** (-0.5)
    devices = lax.axis_size("mode")
    me = lax.axis_index("mode")
    branches, parts, rows, width = branch_in.shape
    quarter = SHARED // width
    holders = devices // (2 * quarter)
    share = rows // (quarter * holders)
    pair = me // (quarter * holders)
    lines = 2 * parts * share
    if lines == 2 * HIGH and holders == KEPT and devices == HIGH * KEPT == width // devices:
        done = run_whole(branch_in, column_order, gate_a, gate_b, devices)
        return done.reshape(2, lines, 2, LANES)
    dealt = branch_in.reshape(2, 2, parts, holders, share, quarter, width)
    dealt = dealt.transpose(0, 5, 3, 2, 1, 4, 6).reshape(devices, parts, 2, share, width)
    orders = lax.dynamic_slice_in_dim(column_order, 2 * pair, 2, 0)
    whole_a = lax.all_gather(gate_a, "mode", axis=1, tiled=True)
    whole_b = lax.all_gather(gate_b, "mode", axis=1, tiled=True)
    dealt = lax.all_to_all(dealt, "mode", split_axis=0, concat_axis=0, tiled=True)
    state = dealt.transpose(1, 0, 2, 3, 4)
    state = layers_plain(state, orders, whole_a, whole_b)

    split = holders // KEPT
    piece = width // split
    free = devices * rows * width // (SHARED * KEPT)
    own_group = [
        [start * holders + h for h in range(holders)] for start in range(2 * quarter)
    ]
    pair_group = [
        [start * quarter * holders + d for d in range(quarter * holders)] for start in range(2)
    ]
    left = state[:, :, 0].reshape(parts, KEPT, devices // KEPT, share, split, piece)
    left = left.transpose(1, 4, 0, 2, 3, 5).reshape(
        holders, parts, devices // KEPT, share, piece
    )
    left = lax.all_to_all(
        left, "mode", split_axis=0, concat_axis=0, tiled=True, axis_index_groups=own_group
    )
    left = left.transpose(1, 2, 0, 3, 4).reshape(parts, free, piece)
    right = state[:, :, 1].reshape(parts, quarter, split, devices // (quarter * split), share, width)
    line = rows * width
    step = KEPT * free
    if width % step == 0:
        several = width // step
        right = right.reshape(
            parts, quarter, split, devices // (quarter * split), share, several, KEPT, free
        )
        right = right.transpose(1, 6, 2, 0, 3, 4, 5, 7)
        right = right.reshape(
            quarter * KEPT * split, parts, devices // (quarter * split), share, several, free
        )
        right = lax.all_to_all(
            right, "mode", split_axis=0, concat_axis=0, tiled=True, axis_index_groups=pair_group
        )
        right = right.reshape(
            quarter, holders, parts, devices // (quarter * split), share, several, free
        )
        right = right.transpose(2, 3, 1, 4, 0, 5, 6).reshape(parts, piece, free)
    else:
        spans = step // width
        kept_row = KEPT // spans
        right = right.reshape(
            parts, quarter, split, devices // (quarter * split), share, kept_row, free
        )
        own_j = me // holders % quarter
        g_high = own_j % spans
        slots = jnp.zeros(
            (quarter, spans, kept_row, split, parts, devices // (quarter * split), share, free), BF16
        )
        filled = right.transpose(1, 5, 2, 0, 3, 4, 6)
        slots = lax.dynamic_update_slice_in_dim(slots, filled[:, None], g_high, 1)
        slots = slots.reshape(
            quarter * KEPT * split, parts, devices // (quarter * split), share, free
        )
        slots = lax.all_to_all(
            slots, "mode", split_axis=0, concat_axis=0, tiled=True, axis_index_groups=pair_group
        )
        slots = slots.reshape(
            quarter // spans, spans, holders, parts, devices // (quarter * split), share, free
        )
        my_g = me % holders // split
        slots = lax.dynamic_index_in_dim(slots, my_g // kept_row, 1, keepdims=False)
        right = slots.transpose(2, 3, 1, 4, 0, 5).reshape(parts, piece, free)
    real_part, imag_part = complex_dot(left[0], left[1], right[0], right[1])
    partial = jnp.stack([real_part, imag_part], axis=1)
    return finish(partial, join_scale, devices, quarter, split)


def finish(partial, join_scale, devices, quarter, split):
    me = lax.axis_index("mode")
    free = partial.shape[0]
    holders = devices // (2 * quarter)
    sum_group = [
        [((p * quarter + j) * KEPT + g) * split + w for j in range(quarter) for w in range(split)]
        for p in range(2)
        for g in range(KEPT)
    ]
    count = quarter * split
    chunks = partial.astype(BF16).reshape(count, free // count, 2, free)
    chunks = lax.all_to_all(
        chunks, "mode", split_axis=0, concat_axis=0, tiled=True, axis_index_groups=sum_group
    )
    done = (jnp.sum(chunks.astype(F32), axis=0) * join_scale).astype(BF16)
    halves = done.reshape(2, free // (2 * count), 2, free)
    pair = me // (quarter * holders)
    same = lax.dynamic_index_in_dim(halves, pair, 0, keepdims=False)
    other = lax.dynamic_index_in_dim(halves, 1 - pair, 0, keepdims=False)
    same_pairs, other_pairs = [], []
    for d in range(devices):
        p, j, g, w = (
            d // (quarter * holders),
            d // holders % quarter,
            d // split % KEPT,
            d % split,
        )
        base = g * (devices // KEPT) + 2 * (j * split + w)
        same_pairs.append((d, base + p))
        other_pairs.append((d, base + 1 - p))
    from_same = lax.ppermute(same, "mode", same_pairs)
    from_other = lax.ppermute(other, "mode", other_pairs)
    parity = me % 2
    first = jnp.where(parity == 0, from_same, from_other)
    second = jnp.where(parity == 0, from_other, from_same)
    return jnp.stack([first, second])


def solution(mesh):
    in_specs = (
        P(None, None, ("cuts", "mode"), None),
        P(),
        P(None, "mode", None),
        P(None, "mode", None),
    )
    out_specs = P(None, ("cuts", "mode"), None, None)
    return jax.shard_map(local, mesh=mesh, in_specs=in_specs, out_specs=out_specs, check_vma=False)
```

```python
import jax
import jax.numpy as jnp
from jax import lax
from jax.experimental import pallas as pl
from jax.experimental.pallas import tpu as pltpu
from jax.sharding import PartitionSpec as P

SHARED = 4096
KEPT = 4
CYCLES = 2
F32 = jnp.float32
BF16 = jnp.bfloat16


def complex_dot(left_real, left_imag, right_real, right_imag):
    real_part = jnp.dot(left_real, right_real, preferred_element_type=F32) - jnp.dot(
        left_imag, right_imag, preferred_element_type=F32
    )
    imag_part = jnp.dot(left_real, right_imag, preferred_element_type=F32) + jnp.dot(
        left_imag, right_real, preferred_element_type=F32
    )
    return real_part, imag_part


def layers_plain(state, orders, whole_a, whole_b):
    parts, devices, sides, share, width = state.shape
    group = width // devices
    iota = lax.broadcasted_iota(jnp.int32, (width, width), 0)
    halves = []
    for side in range(sides):
        one_hot = (iota == orders[side][None, :]).astype(BF16)
        piece = state[:, :, side].reshape(parts * devices * share, width)
        halves.append(
            jnp.dot(piece, one_hot, preferred_element_type=F32)
            .astype(BF16)
            .reshape(parts, devices, share, width)
        )
    state = jnp.stack(halves, axis=2)
    for layer in range(2 * CYCLES):
        if layer > 0:
            pieces = state.reshape(parts, devices, sides, share, devices, group)
            state = pieces.transpose(0, 4, 2, 3, 1, 5)
        flat = state.reshape(parts, devices * sides * share, width)
        gate = whole_a if layer % 2 == 0 else whole_b
        state = jnp.stack(complex_dot(flat[0], flat[1], gate[0], gate[1])).astype(BF16)
    return state.reshape(parts, devices, sides, share, width)


LANES = 128
HIGH = 8


def swap_lane_blocks(blocks, group):
    count = len(blocks)
    lane = lax.broadcasted_iota(jnp.int32, (HIGH, LANES), 1) // group
    bit = count // 2
    while bit:
        low = (lane // bit) % 2 == 0
        new = list(blocks)
        for i in range(count):
            if i & bit == 0:
                first, second = blocks[i], blocks[i | bit]
                new[i] = jnp.where(low, first, pltpu.roll(second, bit * group, 1))
                new[i | bit] = jnp.where(low, pltpu.roll(first, LANES - bit * group, 1), second)
        blocks = new
        bit //= 2
    return blocks


def whole_kernel(
    devices,
    branch,
    order_in,
    gate_a,
    gate_b,
    out,
    gates,
    raw,
    dealt,
    landed,
    state,
    other,
    final,
    product,
    hot,
    comb,
    left_out,
    left_in,
    right,
    part_out,
    part_in,
    orders,
    own_sem,
    relay,
    deal_send,
    deal_recv,
    gate_send,
    gate_recv,
    line_send,
    line_recv,
    left_send,
    left_recv,
    right_send,
    right_recv,
    part_send,
    part_recv,
):
    me = lax.axis_index("mode")
    width = hot.shape[1]
    rows = product.shape[0]
    half = width // 2
    groups = width // devices
    packed = LANES // groups
    share = HIGH // 2
    in_pair = devices // 2
    chips = in_pair // 2
    quarter = SHARED // width
    z, y, x, c = (me // 8, me // 4 % 2, me // 2 % 2, me % 2)
    pair = me // in_pair
    slot = me % in_pair
    first = me - slot
    depth_z = devices // 8
    depth = gates.shape[6]
    every = slice(None)
    shards = (gate_a, gate_b)

    load = pltpu.make_async_copy(branch, raw, own_sem.at[4])
    load.start()
    load_orders = pltpu.make_async_copy(order_in, orders, own_sem.at[3])
    load_orders.start()
    own = [
        pltpu.make_async_copy(shards[g], gates.at[g, :, z, y, x, c], own_sem.at[g])
        for g in range(2)
    ]
    for copy in own:
        copy.start()

    barrier = pltpu.get_barrier_semaphore()
    far = tuple(8 * k for k in range(1, depth_z))
    greeted = tuple(range(1, 8)) + far
    for o in greeted:
        pl.semaphore_signal(barrier, inc=1, device_id={"mode": me ^ o})

    def remote(src, dst, ssem, rsem, target):
        return pltpu.make_async_remote_copy(
            src_ref=src,
            dst_ref=dst,
            send_sem=ssem,
            recv_sem=rsem,
            device_id={"mode": target},
            device_id_type=pl.DeviceIdType.MESH,
        )

    swaps = (
        {
            "p0": (0, y, x, 4),
            "p1": (1, y, x, 2),
            "q0": (0, every, x, 2),
            "q1": (1, y, every, 4),
            "c0": (every, y, x, 1),
            "d0": (0, 1 - y, x, 1),
            "d1": (1, y, 1 - x, 1),
            "e0": (0, every, 1 - x, 1),
            "e1": (1, 1 - y, every, 1),
        },
        {
            "q0": (0, every, x, 2),
            "q1": (1, y, every, 4),
            "d0": (0, every, x, 1),
            "d1": (1, y, every, 1),
            "e0": (0, every, 1 - x, 1),
            "e1": (1, 1 - y, every, 1),
            "p0": (0, y, x, 4),
            "p1": (1, y, x, 2),
        },
    )

    def swap_copy(g, name, place):
        part, at_y, at_x, bit = swaps[g][name]
        here = gates.at[g, part, z + place, at_y, at_x, c]
        first = name in ("p0", "p1", "c0") and place == 0
        src = (shards[g] if name == "c0" else shards[g].at[part]) if first else here
        n = {"p": z + place, "q": depth_z + z + place}.get(name[0], 2 * depth_z)
        return remote(src, here, gate_send.at[g], gate_recv.at[g, n], me ^ bit)

    def on_round(r, action):
        for place in (0,) if r == 0 else (-r, r):
            if place == 0:
                action(place)
            else:

                @pl.when((z + place >= 0) & (z + place < depth_z))
                def _():
                    action(place)

    def send(g, r, *which):
        def action(place):
            for name in which:
                swap_copy(g, name, place).start()

        on_round(r, action)

    def pass_on(g, r, got, which):
        def action(place):
            plane = gates.at[g, :, z + place]
            if got == "p":
                landing(plane.at[:, y, x, c], gate_recv.at[g, z + place])
            else:
                landing(plane.at[:, :, x, c], gate_recv.at[g, depth_z + z + place])
            for name in which:
                swap_copy(g, name, place).start()

        on_round(r, action)

    def landing(ref, sem):
        pltpu.make_async_copy(ref, ref, sem).wait()

    def from_core_end(g):
        landing(gates.at[g, :, :, :, :, 1 - c], gate_recv.at[g, 2 * depth_z])

    def sent(blocks, sem):
        landing(hot.at[:, : blocks * depth // 2], sem)

    threads = ((0, every, y, x), (1, 0, every, x), (1, 1, y, every))

    def line_copy(t, up, k):
        g, part, at_y, at_x = threads[t]
        block = z - k if up else z + k
        here = gates.at[g, part, block, at_y, at_x, c]
        src = shards[0] if t == 0 and k == 0 else here
        return remote(
            src, here, line_send.at[0], line_recv.at[g, block], me + 8 if up else me - 8
        )

    def line_sends(up, k):
        return (z >= k) & (z < depth_z - 1) if up else (z + k < depth_z) & (z > 0)

    def line_gets(up, k):
        return z >= k + 1 if up else z + 1 + k < depth_z

    def line_start(k, *which):
        for up in (1, 0):

            @pl.when(line_sends(up, k))
            def _():
                for t in which:
                    line_copy(t, up, k).start()

    def line_arrive(k, g):
        for up in (1, 0):

            @pl.when(line_gets(up, k))
            def _():
                block = z - 1 - k if up else z + 1 + k
                plane = gates.at[g, :, block]
                landing(
                    plane.at[:, y, x, c] if g == 0 else plane.at[:, :, x, c], line_recv.at[g, block]
                )


    def deal_copy(side, o):
        return remote(
            dealt.at[side, me ^ o],
            landed.at[side, me],
            deal_send.at[side],
            deal_recv.at[side],
            me ^ o,
        )

    def start_deal(side, low, high):
        @pl.loop(low, high)
        def _(o):
            deal_copy(side, o).start()

    def wait_deal(side):
        landing(landed.at[side, : devices - 1], deal_recv.at[side])

    def make_deal(side):
        o = lax.broadcasted_iota(jnp.int32, (rows, rows), 0)
        i = lax.broadcasted_iota(jnp.int32, (rows, rows), 1)
        to, part, own_row = o // HIGH % in_pair, o // share % 2, o % share
        if side == 0:
            q = to % KEPT * in_pair + own_row * quarter + to // KEPT
        else:
            q = to * share + own_row
        source = o // (rows // 2) * (rows // 2) + part * (rows // 4) + q
        pick = jnp.where(i == source, 1.0, 0.0).astype(BF16)
        lines = raw.shape[2]
        for n in range(2):
            block = jnp.concatenate(
                [
                    raw[2 * p + side, part, :, n * half : (n + 1) * half]
                    for p in range(2)
                    for part in range(2)
                ],
                axis=0,
            )
            moved = jnp.dot(pick, block, preferred_element_type=F32)
            product[:, n * half : (n + 1) * half] = moved
        both = [
            product[:, n * half : (n + 1) * half].reshape(devices, HIGH, half) for n in range(2)
        ]
        dealt[side] = jnp.concatenate(both, axis=1).astype(BF16)

    def make_hot(side, k):
        order = orders[pl.ds(2 * pair + side, 1), :]
        span = width // 4
        source = lax.broadcasted_iota(jnp.int32, (span, width), 0) + k * span
        hot[side, pl.ds(k * span, span)] = jnp.where(source == order, 1.0, 0.0).astype(BF16)

    def make_comb(k):
        new = lax.broadcasted_iota(jnp.int32, (1, width), 1)
        natural = (
            new // share % 8 * LANES
            + new // LANES * 16
            + new // 32 % 2 * 8
            + new % share * 2
            + new // 64 % 2
        )
        span = width // 4
        source = lax.broadcasted_iota(jnp.int32, (span, width), 0) + k * span
        comb[pl.ds(k * span, span)] = jnp.where(source == natural, 1.0, 0.0).astype(BF16)

    def relay_signal(k, target):
        pl.semaphore_signal(relay.at[k], inc=1, device_id={"mode": target})

    upper = lax.broadcasted_iota(jnp.int32, (HIGH, LANES), 0) < share
    sign = jnp.where(upper, -1.0, 1.0)

    def turned(block):
        return sign * pltpu.roll(block, share, 0)

    def put(to, at, n, block):
        to[at, n * LANES : (n + 1) * LANES] = block.astype(BF16)
        lines = block.shape[0] // HIGH
        to[at, width + n * LANES : width + (n + 1) * LANES] = jnp.concatenate(
            [turned(block[i * HIGH : (i + 1) * HIGH]) for i in range(lines)], axis=0
        ).astype(BF16)

    span = packed * HIGH
    tile = 2 * LANES
    tiles = [slice(n * tile, (n + 1) * tile) for n in range(width // tile)]

    def take_in(side, to):
        landed[side, pl.ds(me, 1)] = dealt[side, pl.ds(me, 1)]
        wide = landed[side].astype(F32)
        for n in range(2):
            final[:, n * half : (n + 1) * half] = (
                wide[:, n * HIGH : (n + 1) * HIGH].reshape(rows, half).astype(BF16)
            )
        for n, cols in enumerate(tiles):
            moved = jnp.dot(final[...], hot[side, :, cols], preferred_element_type=F32)
            for i in range(rows // span):
                at = slice(i * span, (i + 1) * span)
                for u in range(2):
                    put(to, at, 2 * n + u, moved[at, u * LANES : (u + 1) * LANES])

    def multiplied(g, source, cols):
        block = gates[g, :, :, :, :, :, :, cols].reshape(2 * width, tile)
        return jnp.dot(source[...], block, preferred_element_type=F32)

    def layer(g, source, to):
        for n, cols in enumerate(tiles):
            value = multiplied(g, source, cols)
            for a in range(rows // span):
                for u in range(2):
                    blocks = [
                        value[
                            a * span + i * HIGH : a * span + (i + 1) * HIGH,
                            u * LANES : (u + 1) * LANES,
                        ]
                        for i in range(packed)
                    ]
                    blocks = swap_lane_blocks(blocks, groups)
                    s = 2 * n + u
                    put(to, slice(s * span, (s + 1) * span), a, jnp.concatenate(blocks, axis=0))

    def left_ready(g, source):
        for cols in tiles:
            final[:, cols] = multiplied(g, source, cols).astype(BF16)
        for n, cols in enumerate(tiles):
            moved = jnp.dot(final[...], comb[:, cols], preferred_element_type=F32).astype(BF16)
            for core in range(2):
                for u in range(2):
                    left_out[core, n * 2 + u] = moved[
                        core * (rows // 2) : (core + 1) * (rows // 2), u * LANES : (u + 1) * LANES
                    ]

    def left_copy(o):
        to = slot ^ o
        return remote(
            left_out.at[to % 2, to // 2], left_in.at[slot], left_send.at[0], left_recv.at[0], me ^ o
        )

    own_left = pltpu.make_async_copy(left_out.at[c, slot // 2], left_in.at[slot], own_sem.at[2])

    def right_copy(e):
        return remote(
            right.at[2, :, e], right.at[c, :, e], right_send.at[e], right_recv.at[e], me ^ 1
        )

    def right_ready(g, source):
        for n, cols in enumerate(tiles):
            value = multiplied(g, source, cols)
            for u in range(2):
                e, batch = (2 * n + u) // KEPT, (2 * n + u) % KEPT
                place = jnp.where(batch // 2 == c, c, 2)
                for r in range(devices // 4):
                    lines = [
                        value[
                            (r * 4 + i) * HIGH : (r * 4 + i + 1) * HIGH,
                            u * LANES : (u + 1) * LANES,
                        ]
                        for i in range(4)
                    ]
                    parts = ([], [])
                    for i in range(0, 4, 2):
                        low, top = lines[i], lines[i + 1]
                        parts[0].append(jnp.where(upper, low, pltpu.roll(top, share, 0)))
                        parts[1].append(jnp.where(upper, pltpu.roll(low, share, 0), top))
                    for part in range(2):
                        right[place, part, e, batch % 2, r * 16 : (r + 1) * 16] = jnp.concatenate(
                            parts[part], axis=0
                        ).astype(BF16)
            if (2 * n + 2) % KEPT == 0:
                right_copy((2 * n + 1) // KEPT).start()

    def join(then):
        for g in range(2):
            at = slice(g * (rows // 4), (g + 1) * (rows // 4))
            lefts = jnp.concatenate(
                [
                    jnp.concatenate([left_in[j * KEPT + h, at] for j in range(quarter)], axis=1)
                    for h in range(KEPT)
                ],
                axis=0,
            )
            step = devices
            rights = jnp.concatenate(
                [
                    jnp.concatenate(
                        [right[core, part, e, g, j * step : (j + 1) * step] for part in range(2)],
                        axis=1,
                    )
                    for j in range(quarter)
                    for e in range(2)
                    for core in range(2)
                ],
                axis=0,
            )
            both = jnp.dot(lefts, rights, preferred_element_type=F32)
            span = rows // KEPT
            for a in range(HIGH):
                lines = []
                for h in range(0, KEPT, 2):
                    low = both[h * span + a * HIGH : h * span + (a + 1) * HIGH]
                    top = both[(h + 1) * span + a * HIGH : (h + 1) * span + (a + 1) * HIGH]
                    a0, b0, a1, b1 = (low[:, :LANES], low[:, LANES:], top[:, :LANES], top[:, LANES:])
                    real = jnp.where(
                        upper, a0 - pltpu.roll(b0, share, 0), pltpu.roll(a1, share, 0) - b1
                    )
                    imag = jnp.where(
                        upper, b0 + pltpu.roll(a0, share, 0), pltpu.roll(b1, share, 0) + a1
                    )
                    lines.append(jnp.concatenate([real, imag], axis=1))
                part_out[g * HIGH + a] = jnp.concatenate(lines, axis=0).astype(BF16)
            then(g)

    from_chip = me // 2

    def part_copy(i):
        return remote(
            part_out.at[i],
            part_in.at[from_chip],
            part_send.at[0],
            part_recv.at[0],
            c * in_pair + i,
        )

    own_part = pltpu.make_async_copy(part_out.at[slot], part_in.at[from_chip], part_recv.at[0])

    through = ("q0", "q1", "d0", "d1")
    start = ("p0", "p1", "c0")

    def first_a(r):
        line_arrive(r - 1, 0)
        if r < depth_z - 1:
            line_start(r, 0)
        send(0, r, *start)

    def second_a(r):
        pass_on(0, r, "p", through)

    def third(g, r):
        pass_on(g, r, "q", ("e0", "e1"))

    def first_b(r):
        line_arrive(r - 1, 1)
        if r < depth_z - 1:
            line_start(r, 1, 2)
        send(1, r, *through)

    def finish_phase_a():
        each_a, each_b = 14, 12
        sent(each_a * depth_z, gate_send.at[0])
        sent(each_b * depth_z + 2, gate_send.at[1])
        inner = (z > 0) & (z < depth_z - 1)

        @pl.when(inner)
        def _():
            sent(6 * (depth_z + 1), line_send.at[0])

        @pl.when(jnp.logical_not(inner))
        def _():
            sent(6, line_send.at[0])

        for side in range(2):
            landing(dealt.at[side, : devices - 1], deal_send.at[side])

    pl.semaphore_wait(barrier, len(greeted))
    line_start(0, 0)
    send(1, 0, "p0", "p1")
    send(0, 0, *start)
    for k, o in enumerate(far):
        relay_signal(k, me ^ o)
    load.wait()
    make_deal(0)
    make_deal(1)
    own[0].wait()
    own[1].wait()
    pass_on(1, 0, "p", ())
    line_start(0, 1, 2)
    first_a(1)
    second_a(0)
    send(1, 0, *through)
    for k in range(len(far)):
        pl.semaphore_wait(relay.at[k], 1)
    start_deal(0, 1, 9)
    first_a(2)
    start_deal(0, 9, 17)
    first_b(1)
    second_a(1)
    start_deal(0, 17, 25)
    first_a(3)
    third(0, 0)
    start_deal(0, 25, 32)
    second_a(2)
    first_b(2)
    third(1, 0)
    third(0, 1)
    second_a(3)
    first_b(3)
    third(1, 1)
    third(0, 2)
    start_deal(1, 16, 32)
    load_orders.wait()
    for k in range(4):
        make_hot(0, k)
    third(0, 3)
    third(1, 2)
    third(1, 3)
    start_deal(1, 1, 16)
    for k in range(4):
        make_hot(1, k)
        make_comb(k)
    wait_deal(0)
    take_in(0, state)
    from_core_end(0)
    layer(0, state, other)
    from_core_end(1)
    layer(1, other, state)
    layer(0, state, other)
    left_ready(1, other)

    @pl.loop(1, in_pair)
    def _(o):
        left_copy(o).start()

    own_left.start()
    wait_deal(1)
    take_in(1, state)
    layer(0, state, other)
    layer(1, other, state)
    layer(0, state, other)
    right_ready(1, other)
    own_left.wait()

    landing(left_in.at[: in_pair - 1], left_recv.at[0])

    for e in range(2):
        right_copy(e).wait()
    def send_parts(g):
        @pl.loop(g * HIGH, (g + 1) * HIGH)
        def _(i):
            target = c * in_pair + i

            @pl.when(target != me)
            def _():
                part_copy(i).start()

            @pl.when(target == me)
            def _():
                own_part.start()

    join(send_parts)
    landing(part_in, part_recv.at[0])
    scale = (2.0 * SHARED) ** (-0.5)
    for p in range(2):
        total = part_in[p * chips].astype(F32)
        for i in range(1, chips):
            total += part_in[p * chips + i].astype(F32)
        out[p] = (total * scale).astype(BF16)

    @pl.when(me // in_pair == c)
    def _():
        landing(part_out.at[: in_pair - 1], part_send.at[0])

    @pl.when(me // in_pair != c)
    def _():
        landing(part_out, part_send.at[0])

    landing(left_in.at[: in_pair - 1], left_send.at[0])
    finish_phase_a()


def run_whole(branch, orders, gate_a, gate_b, devices):
    width = branch.shape[3]
    depth = gate_a.shape[1]
    rows = devices * HIGH
    lines = 2 * HIGH
    in_pair = devices // 2
    dma = pltpu.SemaphoreType.DMA
    vmem = pl.BlockSpec(memory_space=pltpu.VMEM)
    hbm = pl.BlockSpec(memory_space=pl.ANY)
    return pl.pallas_call(
        lambda *refs: whole_kernel(devices, *refs),
        out_shape=jax.ShapeDtypeStruct((2, lines, 2 * LANES), BF16),
        in_specs=[hbm] * 4,
        out_specs=vmem,
        scratch_shapes=[
            pltpu.VMEM((2, 2, devices // 8, 2, 2, 2, depth, width), BF16),
            pltpu.VMEM(branch.shape, BF16),
            pltpu.VMEM((2, devices, lines, width // 2), BF16),
            pltpu.VMEM((2, devices, lines, width // 2), BF16),
            pltpu.VMEM((rows, 2 * width), BF16),
            pltpu.VMEM((rows, 2 * width), BF16),
            pltpu.VMEM((rows, width), BF16),
            pltpu.VMEM((rows, width), F32),
            pltpu.VMEM((2, width, width), BF16),
            pltpu.VMEM((width, width), BF16),
            pltpu.VMEM((2, in_pair // 2, rows // 2, LANES), BF16),
            pltpu.VMEM((in_pair, rows // 2, LANES), BF16),
            pltpu.VMEM((3, 2, 2, 2, rows // 2, LANES), BF16),
            pltpu.VMEM((in_pair, lines, 2 * LANES), BF16),
            pltpu.VMEM((in_pair, lines, 2 * LANES), BF16),
            pltpu.VMEM(orders.shape, jnp.int32),
            dma((5,)),
            pltpu.SemaphoreType.REGULAR((devices // 8 - 1,)),
            dma((2,)),
            dma((2,)),
            dma((2,)),
            dma((2, 2 * (devices // 8) + 1)),
            dma((1,)),
            dma((2, devices // 8)),
            dma((1,)),
            dma((1,)),
            dma((2,)),
            dma((2,)),
            dma((1,)),
            dma((1,)),
        ],
        compiler_params=pltpu.CompilerParams(
            collective_id=0, has_side_effects=True, vmem_limit_bytes=60 * 2**20
        ),
    )(branch, orders, gate_a, gate_b)


def local(branch_in, column_order, gate_a, gate_b):
    join_scale = (2.0 * SHARED) ** (-0.5)
    devices = lax.axis_size("mode")
    me = lax.axis_index("mode")
    branches, parts, rows, width = branch_in.shape
    quarter = SHARED // width
    holders = devices // (2 * quarter)
    share = rows // (quarter * holders)
    pair = me // (quarter * holders)
    lines = 2 * parts * share
    if lines == 2 * HIGH and holders == KEPT and devices == HIGH * KEPT == width // devices:
        done = run_whole(branch_in, column_order, gate_a, gate_b, devices)
        return done.reshape(2, lines, 2, LANES)
    dealt = branch_in.reshape(2, 2, parts, holders, share, quarter, width)
    dealt = dealt.transpose(0, 5, 3, 2, 1, 4, 6).reshape(devices, parts, 2, share, width)
    orders = lax.dynamic_slice_in_dim(column_order, 2 * pair, 2, 0)
    whole_a = lax.all_gather(gate_a, "mode", axis=1, tiled=True)
    whole_b = lax.all_gather(gate_b, "mode", axis=1, tiled=True)
    dealt = lax.all_to_all(dealt, "mode", split_axis=0, concat_axis=0, tiled=True)
    state = dealt.transpose(1, 0, 2, 3, 4)
    state = layers_plain(state, orders, whole_a, whole_b)

    split = holders // KEPT
    piece = width // split
    free = devices * rows * width // (SHARED * KEPT)
    own_group = [
        [start * holders + h for h in range(holders)] for start in range(2 * quarter)
    ]
    pair_group = [
        [start * quarter * holders + d for d in range(quarter * holders)] for start in range(2)
    ]
    left = state[:, :, 0].reshape(parts, KEPT, devices // KEPT, share, split, piece)
    left = left.transpose(1, 4, 0, 2, 3, 5).reshape(
        holders, parts, devices // KEPT, share, piece
    )
    left = lax.all_to_all(
        left, "mode", split_axis=0, concat_axis=0, tiled=True, axis_index_groups=own_group
    )
    left = left.transpose(1, 2, 0, 3, 4).reshape(parts, free, piece)
    right = state[:, :, 1].reshape(parts, quarter, split, devices // (quarter * split), share, width)
    line = rows * width
    step = KEPT * free
    if width % step == 0:
        several = width // step
        right = right.reshape(
            parts, quarter, split, devices // (quarter * split), share, several, KEPT, free
        )
        right = right.transpose(1, 6, 2, 0, 3, 4, 5, 7)
        right = right.reshape(
            quarter * KEPT * split, parts, devices // (quarter * split), share, several, free
        )
        right = lax.all_to_all(
            right, "mode", split_axis=0, concat_axis=0, tiled=True, axis_index_groups=pair_group
        )
        right = right.reshape(
            quarter, holders, parts, devices // (quarter * split), share, several, free
        )
        right = right.transpose(2, 3, 1, 4, 0, 5, 6).reshape(parts, piece, free)
    else:
        spans = step // width
        kept_row = KEPT // spans
        right = right.reshape(
            parts, quarter, split, devices // (quarter * split), share, kept_row, free
        )
        own_j = me // holders % quarter
        g_high = own_j % spans
        slots = jnp.zeros(
            (quarter, spans, kept_row, split, parts, devices // (quarter * split), share, free), BF16
        )
        filled = right.transpose(1, 5, 2, 0, 3, 4, 6)
        slots = lax.dynamic_update_slice_in_dim(slots, filled[:, None], g_high, 1)
        slots = slots.reshape(
            quarter * KEPT * split, parts, devices // (quarter * split), share, free
        )
        slots = lax.all_to_all(
            slots, "mode", split_axis=0, concat_axis=0, tiled=True, axis_index_groups=pair_group
        )
        slots = slots.reshape(
            quarter // spans, spans, holders, parts, devices // (quarter * split), share, free
        )
        my_g = me % holders // split
        slots = lax.dynamic_index_in_dim(slots, my_g // kept_row, 1, keepdims=False)
        right = slots.transpose(2, 3, 1, 4, 0, 5).reshape(parts, piece, free)
    real_part, imag_part = complex_dot(left[0], left[1], right[0], right[1])
    partial = jnp.stack([real_part, imag_part], axis=1)
    return finish(partial, join_scale, devices, quarter, split)


def finish(partial, join_scale, devices, quarter, split):
    me = lax.axis_index("mode")
    free = partial.shape[0]
    holders = devices // (2 * quarter)
    sum_group = [
        [((p * quarter + j) * KEPT + g) * split + w for j in range(quarter) for w in range(split)]
        for p in range(2)
        for g in range(KEPT)
    ]
    count = quarter * split
    chunks = partial.astype(BF16).reshape(count, free // count, 2, free)
    chunks = lax.all_to_all(
        chunks, "mode", split_axis=0, concat_axis=0, tiled=True, axis_index_groups=sum_group
    )
    done = (jnp.sum(chunks.astype(F32), axis=0) * join_scale).astype(BF16)
    halves = done.reshape(2, free // (2 * count), 2, free)
    pair = me // (quarter * holders)
    same = lax.dynamic_index_in_dim(halves, pair, 0, keepdims=False)
    other = lax.dynamic_index_in_dim(halves, 1 - pair, 0, keepdims=False)
    same_pairs, other_pairs = [], []
    for d in range(devices):
        p, j, g, w = (
            d // (quarter * holders),
            d // holders % quarter,
            d // split % KEPT,
            d % split,
        )
        base = g * (devices // KEPT) + 2 * (j * split + w)
        same_pairs.append((d, base + p))
        other_pairs.append((d, base + 1 - p))
    from_same = lax.ppermute(same, "mode", same_pairs)
    from_other = lax.ppermute(other, "mode", other_pairs)
    parity = me % 2
    first = jnp.where(parity == 0, from_same, from_other)
    second = jnp.where(parity == 0, from_other, from_same)
    return jnp.stack([first, second])


def solution(mesh):
    in_specs = (
        P(None, None, ("cuts", "mode"), None),
        P(),
        P(None, "mode", None),
        P(None, "mode", None),
    )
    out_specs = P(None, ("cuts", "mode"), None, None)
    return jax.shard_map(local, mesh=mesh, in_specs=in_specs, out_specs=out_specs, check_vma=False)
```

```python
import jax
import jax.numpy as jnp
from jax import lax
from jax.experimental import pallas as pl
from jax.experimental.pallas import tpu as pltpu
from jax.sharding import PartitionSpec as P

SHARED = 4096
KEPT = 4
CYCLES = 2
F32 = jnp.float32
BF16 = jnp.bfloat16


def complex_dot(left_real, left_imag, right_real, right_imag):
    real_part = jnp.dot(left_real, right_real, preferred_element_type=F32) - jnp.dot(
        left_imag, right_imag, preferred_element_type=F32
    )
    imag_part = jnp.dot(left_real, right_imag, preferred_element_type=F32) + jnp.dot(
        left_imag, right_real, preferred_element_type=F32
    )
    return real_part, imag_part


def layers_plain(state, orders, whole_a, whole_b):
    parts, devices, sides, share, width = state.shape
    group = width // devices
    iota = lax.broadcasted_iota(jnp.int32, (width, width), 0)
    halves = []
    for side in range(sides):
        one_hot = (iota == orders[side][None, :]).astype(BF16)
        piece = state[:, :, side].reshape(parts * devices * share, width)
        halves.append(
            jnp.dot(piece, one_hot, preferred_element_type=F32)
            .astype(BF16)
            .reshape(parts, devices, share, width)
        )
    state = jnp.stack(halves, axis=2)
    for layer in range(2 * CYCLES):
        if layer > 0:
            pieces = state.reshape(parts, devices, sides, share, devices, group)
            state = pieces.transpose(0, 4, 2, 3, 1, 5)
        flat = state.reshape(parts, devices * sides * share, width)
        gate = whole_a if layer % 2 == 0 else whole_b
        state = jnp.stack(complex_dot(flat[0], flat[1], gate[0], gate[1])).astype(BF16)
    return state.reshape(parts, devices, sides, share, width)


LANES = 128
HIGH = 8


def swap_lane_blocks(blocks, group):
    count = len(blocks)
    lane = lax.broadcasted_iota(jnp.int32, (HIGH, LANES), 1) // group
    bit = count // 2
    while bit:
        low = (lane // bit) % 2 == 0
        new = list(blocks)
        for i in range(count):
            if i & bit == 0:
                first, second = blocks[i], blocks[i | bit]
                new[i] = jnp.where(low, first, pltpu.roll(second, bit * group, 1))
                new[i | bit] = jnp.where(low, pltpu.roll(first, LANES - bit * group, 1), second)
        blocks = new
        bit //= 2
    return blocks


def whole_kernel(
    devices,
    branch,
    order_in,
    gate_a,
    gate_b,
    out,
    gates,
    raw,
    dealt,
    landed,
    state,
    other,
    final,
    product,
    hot,
    comb,
    left_out,
    left_in,
    right,
    part_out,
    part_in,
    orders,
    own_sem,
    relay,
    deal_send,
    deal_recv,
    gate_send,
    gate_recv,
    line_send,
    line_recv,
    left_send,
    left_recv,
    right_send,
    right_recv,
    part_send,
    part_recv,
):
    me = lax.axis_index("mode")
    width = hot.shape[1]
    rows = product.shape[0]
    half = width // 2
    groups = width // devices
    packed = LANES // groups
    share = HIGH // 2
    in_pair = devices // 2
    chips = in_pair // 2
    quarter = SHARED // width
    z, y, x, c = (me // 8, me // 4 % 2, me // 2 % 2, me % 2)
    pair = me // in_pair
    slot = me % in_pair
    first = me - slot
    depth_z = devices // 8
    depth = gates.shape[6]
    every = slice(None)
    shards = (gate_a, gate_b)

    load = pltpu.make_async_copy(branch, raw, own_sem.at[4])
    load.start()
    load_orders = pltpu.make_async_copy(order_in, orders, own_sem.at[3])
    load_orders.start()
    own = [
        pltpu.make_async_copy(shards[g], gates.at[g, :, z, y, x, c], own_sem.at[g])
        for g in range(2)
    ]
    for copy in own:
        copy.start()

    barrier = pltpu.get_barrier_semaphore()
    far = tuple(8 * k for k in range(1, depth_z))
    greeted = tuple(range(1, 8)) + far
    for o in greeted:
        pl.semaphore_signal(barrier, inc=1, device_id={"mode": me ^ o})

    def remote(src, dst, ssem, rsem, target):
        return pltpu.make_async_remote_copy(
            src_ref=src,
            dst_ref=dst,
            send_sem=ssem,
            recv_sem=rsem,
            device_id={"mode": target},
            device_id_type=pl.DeviceIdType.MESH,
        )

    swaps = (
        {
            "p0": (0, y, x, 4),
            "p1": (1, y, x, 2),
            "q0": (0, every, x, 2),
            "q1": (1, y, every, 4),
            "c0": (every, y, x, 1),
            "d0": (0, 1 - y, x, 1),
            "d1": (1, y, 1 - x, 1),
            "e0": (0, every, 1 - x, 1),
            "e1": (1, 1 - y, every, 1),
        },
        {
            "q0": (0, every, x, 2),
            "q1": (1, y, every, 4),
            "d0": (0, every, x, 1),
            "d1": (1, y, every, 1),
            "e0": (0, every, 1 - x, 1),
            "e1": (1, 1 - y, every, 1),
            "p0": (0, y, x, 4),
            "p1": (1, y, x, 2),
        },
    )

    def swap_copy(g, name, place):
        part, at_y, at_x, bit = swaps[g][name]
        here = gates.at[g, part, z + place, at_y, at_x, c]
        first = name in ("p0", "p1", "c0") and place == 0
        src = (shards[g] if name == "c0" else shards[g].at[part]) if first else here
        n = {"p": z + place, "q": depth_z + z + place}.get(name[0], 2 * depth_z)
        return remote(src, here, gate_send.at[g], gate_recv.at[g, n], me ^ bit)

    def on_round(r, action):
        for place in (0,) if r == 0 else (-r, r):
            if place == 0:
                action(place)
            else:

                @pl.when((z + place >= 0) & (z + place < depth_z))
                def _():
                    action(place)

    def send(g, r, *which):
        def action(place):
            for name in which:
                swap_copy(g, name, place).start()

        on_round(r, action)

    def pass_on(g, r, got, which):
        def action(place):
            plane = gates.at[g, :, z + place]
            if got == "p":
                landing(plane.at[:, y, x, c], gate_recv.at[g, z + place])
            else:
                landing(plane.at[:, :, x, c], gate_recv.at[g, depth_z + z + place])
            for name in which:
                swap_copy(g, name, place).start()

        on_round(r, action)

    def landing(ref, sem):
        pltpu.make_async_copy(ref, ref, sem).wait()

    def from_core_end(g):
        landing(gates.at[g, :, :, :, :, 1 - c], gate_recv.at[g, 2 * depth_z])

    def sent(blocks, sem):
        landing(hot.at[:, : blocks * depth // 2], sem)

    threads = ((0, every, y, x), (1, 0, every, x), (1, 1, y, every))

    def line_copy(t, up, k):
        g, part, at_y, at_x = threads[t]
        block = z - k if up else z + k
        here = gates.at[g, part, block, at_y, at_x, c]
        src = shards[0] if t == 0 and k == 0 else here
        return remote(
            src, here, line_send.at[0], line_recv.at[g, block], me + 8 if up else me - 8
        )

    def line_sends(up, k):
        return (z >= k) & (z < depth_z - 1) if up else (z + k < depth_z) & (z > 0)

    def line_gets(up, k):
        return z >= k + 1 if up else z + 1 + k < depth_z

    def line_start(k, *which):
        for up in (1, 0):

            @pl.when(line_sends(up, k))
            def _():
                for t in which:
                    line_copy(t, up, k).start()

    def line_arrive(k, g):
        for up in (1, 0):

            @pl.when(line_gets(up, k))
            def _():
                block = z - 1 - k if up else z + 1 + k
                plane = gates.at[g, :, block]
                landing(
                    plane.at[:, y, x, c] if g == 0 else plane.at[:, :, x, c], line_recv.at[g, block]
                )


    def deal_copy(side, o):
        return remote(
            dealt.at[side, me ^ o],
            landed.at[side, me],
            deal_send.at[side],
            deal_recv.at[side],
            me ^ o,
        )

    def start_deal(side, low, high):
        @pl.loop(low, high)
        def _(o):
            deal_copy(side, o).start()

    def wait_deal(side):
        landing(landed.at[side, : devices - 1], deal_recv.at[side])

    def make_deal(side):
        o = lax.broadcasted_iota(jnp.int32, (rows, rows), 0)
        i = lax.broadcasted_iota(jnp.int32, (rows, rows), 1)
        to, part, own_row = o // HIGH % in_pair, o // share % 2, o % share
        if side == 0:
            q = to % KEPT * in_pair + own_row * quarter + to // KEPT
        else:
            q = to * share + own_row
        source = o // (rows // 2) * (rows // 2) + part * (rows // 4) + q
        pick = jnp.where(i == source, 1.0, 0.0).astype(BF16)
        lines = raw.shape[2]
        for n in range(2):
            block = jnp.concatenate(
                [
                    raw[2 * p + side, part, :, n * half : (n + 1) * half]
                    for p in range(2)
                    for part in range(2)
                ],
                axis=0,
            )
            moved = jnp.dot(pick, block, preferred_element_type=F32)
            product[:, n * half : (n + 1) * half] = moved
        both = [
            product[:, n * half : (n + 1) * half].reshape(devices, HIGH, half) for n in range(2)
        ]
        dealt[side] = jnp.concatenate(both, axis=1).astype(BF16)

    def make_hot(side, k):
        order = orders[pl.ds(2 * pair + side, 1), :]
        span = width // 4
        source = lax.broadcasted_iota(jnp.int32, (span, width), 0) + k * span
        hot[side, pl.ds(k * span, span)] = jnp.where(source == order, 1.0, 0.0).astype(BF16)

    def make_comb(k):
        new = lax.broadcasted_iota(jnp.int32, (1, width), 1)
        natural = (
            new // share % 8 * LANES
            + new // LANES * 16
            + new // 32 % 2 * 8
            + new % share * 2
            + new // 64 % 2
        )
        span = width // 4
        source = lax.broadcasted_iota(jnp.int32, (span, width), 0) + k * span
        comb[pl.ds(k * span, span)] = jnp.where(source == natural, 1.0, 0.0).astype(BF16)

    def relay_signal(k, target):
        pl.semaphore_signal(relay.at[k], inc=1, device_id={"mode": target})

    upper = lax.broadcasted_iota(jnp.int32, (HIGH, LANES), 0) < share
    sign = jnp.where(upper, -1.0, 1.0)

    def turned(block):
        return sign * pltpu.roll(block, share, 0)

    def put(to, at, n, block):
        to[at, n * LANES : (n + 1) * LANES] = block.astype(BF16)
        lines = block.shape[0] // HIGH
        to[at, width + n * LANES : width + (n + 1) * LANES] = jnp.concatenate(
            [turned(block[i * HIGH : (i + 1) * HIGH]) for i in range(lines)], axis=0
        ).astype(BF16)

    span = packed * HIGH
    tile = 2 * LANES
    tiles = [slice(n * tile, (n + 1) * tile) for n in range(width // tile)]

    def take_in(side, to):
        landed[side, pl.ds(me, 1)] = dealt[side, pl.ds(me, 1)]
        wide = landed[side].astype(F32)
        for n in range(2):
            final[:, n * half : (n + 1) * half] = (
                wide[:, n * HIGH : (n + 1) * HIGH].reshape(rows, half).astype(BF16)
            )
        for n, cols in enumerate(tiles):
            moved = jnp.dot(final[...], hot[side, :, cols], preferred_element_type=F32)
            for i in range(rows // span):
                at = slice(i * span, (i + 1) * span)
                for u in range(2):
                    put(to, at, 2 * n + u, moved[at, u * LANES : (u + 1) * LANES])

    def multiplied(g, source, cols):
        block = gates[g, :, :, :, :, :, :, cols].reshape(2 * width, tile)
        return jnp.dot(source[...], block, preferred_element_type=F32)

    def layer(g, source, to):
        for n, cols in enumerate(tiles):
            value = multiplied(g, source, cols)
            for a in range(rows // span):
                for u in range(2):
                    blocks = [
                        value[
                            a * span + i * HIGH : a * span + (i + 1) * HIGH,
                            u * LANES : (u + 1) * LANES,
                        ]
                        for i in range(packed)
                    ]
                    blocks = swap_lane_blocks(blocks, groups)
                    s = 2 * n + u
                    put(to, slice(s * span, (s + 1) * span), a, jnp.concatenate(blocks, axis=0))

    def left_ready(g, source):
        for cols in tiles:
            final[:, cols] = multiplied(g, source, cols).astype(BF16)
        for n, cols in enumerate(tiles):
            moved = jnp.dot(final[...], comb[:, cols], preferred_element_type=F32).astype(BF16)
            for core in range(2):
                for u in range(2):
                    left_out[core, n * 2 + u] = moved[
                        core * (rows // 2) : (core + 1) * (rows // 2), u * LANES : (u + 1) * LANES
                    ]

    def left_copy(o):
        to = slot ^ o
        return remote(
            left_out.at[to % 2, to // 2], left_in.at[slot], left_send.at[0], left_recv.at[0], me ^ o
        )

    own_left = pltpu.make_async_copy(left_out.at[c, slot // 2], left_in.at[slot], own_sem.at[2])

    def right_copy(e):
        return remote(
            right.at[2, :, e], right.at[c, :, e], right_send.at[e], right_recv.at[e], me ^ 1
        )

    def right_ready(g, source):
        for n, cols in enumerate(tiles):
            value = multiplied(g, source, cols)
            for u in range(2):
                e, batch = (2 * n + u) // KEPT, (2 * n + u) % KEPT
                place = jnp.where(batch // 2 == c, c, 2)
                for r in range(devices // 4):
                    lines = [
                        value[
                            (r * 4 + i) * HIGH : (r * 4 + i + 1) * HIGH,
                            u * LANES : (u + 1) * LANES,
                        ]
                        for i in range(4)
                    ]
                    parts = ([], [])
                    for i in range(0, 4, 2):
                        low, top = lines[i], lines[i + 1]
                        parts[0].append(jnp.where(upper, low, pltpu.roll(top, share, 0)))
                        parts[1].append(jnp.where(upper, pltpu.roll(low, share, 0), top))
                    for part in range(2):
                        right[place, part, e, batch % 2, r * 16 : (r + 1) * 16] = jnp.concatenate(
                            parts[part], axis=0
                        ).astype(BF16)
            if (2 * n + 2) % KEPT == 0:
                right_copy((2 * n + 1) // KEPT).start()

    def join(then):
        for g in range(2):
            at = slice(g * (rows // 4), (g + 1) * (rows // 4))
            lefts = jnp.concatenate(
                [
                    jnp.concatenate([left_in[j * KEPT + h, at] for j in range(quarter)], axis=1)
                    for h in range(KEPT)
                ],
                axis=0,
            )
            step = devices
            rights = jnp.concatenate(
                [
                    jnp.concatenate(
                        [right[core, part, e, g, j * step : (j + 1) * step] for part in range(2)],
                        axis=1,
                    )
                    for j in range(quarter)
                    for e in range(2)
                    for core in range(2)
                ],
                axis=0,
            )
            both = jnp.dot(lefts, rights, preferred_element_type=F32)
            span = rows // KEPT
            for a in range(HIGH):
                lines = []
                for h in range(0, KEPT, 2):
                    low = both[h * span + a * HIGH : h * span + (a + 1) * HIGH]
                    top = both[(h + 1) * span + a * HIGH : (h + 1) * span + (a + 1) * HIGH]
                    a0, b0, a1, b1 = (low[:, :LANES], low[:, LANES:], top[:, :LANES], top[:, LANES:])
                    real = jnp.where(
                        upper, a0 - pltpu.roll(b0, share, 0), pltpu.roll(a1, share, 0) - b1
                    )
                    imag = jnp.where(
                        upper, b0 + pltpu.roll(a0, share, 0), pltpu.roll(b1, share, 0) + a1
                    )
                    lines.append(jnp.concatenate([real, imag], axis=1))
                part_out[g * HIGH + a] = jnp.concatenate(lines, axis=0).astype(BF16)
            then(g)

    from_chip = me // 2

    def part_copy(i):
        return remote(
            part_out.at[i],
            part_in.at[from_chip],
            part_send.at[0],
            part_recv.at[0],
            c * in_pair + i,
        )

    own_part = pltpu.make_async_copy(part_out.at[slot], part_in.at[from_chip], part_recv.at[0])

    through = ("q0", "q1", "d0", "d1")
    start = ("p0", "p1", "c0")

    def first_a(r):
        line_arrive(r - 1, 0)
        if r < depth_z - 1:
            line_start(r, 0)
        send(0, r, *start)

    def second_a(r):
        pass_on(0, r, "p", through)

    def third(g, r):
        pass_on(g, r, "q", ("e0", "e1"))

    def first_b(r):
        line_arrive(r - 1, 1)
        if r < depth_z - 1:
            line_start(r, 1, 2)
        send(1, r, *through)

    def finish_phase_a():
        each_a, each_b = 14, 12
        sent(each_a * depth_z, gate_send.at[0])
        sent(each_b * depth_z + 2, gate_send.at[1])
        inner = (z > 0) & (z < depth_z - 1)

        @pl.when(inner)
        def _():
            sent(6 * (depth_z + 1), line_send.at[0])

        @pl.when(jnp.logical_not(inner))
        def _():
            sent(6, line_send.at[0])

        for side in range(2):
            landing(dealt.at[side, : devices - 1], deal_send.at[side])

    pl.semaphore_wait(barrier, len(greeted))
    line_start(0, 0)
    send(1, 0, "p0", "p1")
    send(0, 0, *start)
    for k, o in enumerate(far):
        relay_signal(k, me ^ o)
    load.wait()
    make_deal(0)
    make_deal(1)
    own[0].wait()
    own[1].wait()
    pass_on(1, 0, "p", ())
    line_start(0, 1, 2)
    first_a(1)
    second_a(0)
    send(1, 0, *through)
    for k in range(len(far)):
        pl.semaphore_wait(relay.at[k], 1)
    start_deal(0, 1, 9)
    first_a(2)
    start_deal(0, 9, 17)
    first_b(1)
    second_a(1)
    start_deal(0, 17, 25)
    first_a(3)
    third(0, 0)
    start_deal(0, 25, 32)
    second_a(2)
    first_b(2)
    third(1, 0)
    third(0, 1)
    second_a(3)
    first_b(3)
    third(1, 1)
    third(0, 2)
    start_deal(1, 16, 32)
    load_orders.wait()
    for k in range(4):
        make_hot(0, k)
    third(0, 3)
    third(1, 2)
    third(1, 3)
    start_deal(1, 1, 16)
    for k in range(4):
        make_hot(1, k)
        make_comb(k)
    wait_deal(0)
    take_in(0, state)
    from_core_end(0)
    layer(0, state, other)
    from_core_end(1)
    layer(1, other, state)
    layer(0, state, other)
    left_ready(1, other)

    @pl.loop(1, in_pair)
    def _(o):
        left_copy(o).start()

    own_left.start()
    wait_deal(1)
    take_in(1, state)
    layer(0, state, other)
    layer(1, other, state)
    layer(0, state, other)
    right_ready(1, other)
    own_left.wait()

    landing(left_in.at[: in_pair - 1], left_recv.at[0])

    for e in range(2):
        right_copy(e).wait()
    def send_parts(g):
        @pl.loop(g * HIGH, (g + 1) * HIGH)
        def _(i):
            target = c * in_pair + i

            @pl.when(target != me)
            def _():
                part_copy(i).start()

            @pl.when(target == me)
            def _():
                own_part.start()

    join(send_parts)
    landing(left_in.at[: in_pair - 1], left_send.at[0])
    finish_phase_a()
    landing(part_in, part_recv.at[0])
    scale = (2.0 * SHARED) ** (-0.5)
    for p in range(2):
        total = part_in[p * chips].astype(F32)
        for i in range(1, chips):
            total += part_in[p * chips + i].astype(F32)
        out[p] = (total * scale).astype(BF16)

    @pl.when(me // in_pair == c)
    def _():
        landing(part_out.at[: in_pair - 1], part_send.at[0])

    @pl.when(me // in_pair != c)
    def _():
        landing(part_out, part_send.at[0])


def run_whole(branch, orders, gate_a, gate_b, devices):
    width = branch.shape[3]
    depth = gate_a.shape[1]
    rows = devices * HIGH
    lines = 2 * HIGH
    in_pair = devices // 2
    dma = pltpu.SemaphoreType.DMA
    vmem = pl.BlockSpec(memory_space=pltpu.VMEM)
    hbm = pl.BlockSpec(memory_space=pl.ANY)
    return pl.pallas_call(
        lambda *refs: whole_kernel(devices, *refs),
        out_shape=jax.ShapeDtypeStruct((2, lines, 2 * LANES), BF16),
        in_specs=[hbm] * 4,
        out_specs=vmem,
        scratch_shapes=[
            pltpu.VMEM((2, 2, devices // 8, 2, 2, 2, depth, width), BF16),
            pltpu.VMEM(branch.shape, BF16),
            pltpu.VMEM((2, devices, lines, width // 2), BF16),
            pltpu.VMEM((2, devices, lines, width // 2), BF16),
            pltpu.VMEM((rows, 2 * width), BF16),
            pltpu.VMEM((rows, 2 * width), BF16),
            pltpu.VMEM((rows, width), BF16),
            pltpu.VMEM((rows, width), F32),
            pltpu.VMEM((2, width, width), BF16),
            pltpu.VMEM((width, width), BF16),
            pltpu.VMEM((2, in_pair // 2, rows // 2, LANES), BF16),
            pltpu.VMEM((in_pair, rows // 2, LANES), BF16),
            pltpu.VMEM((3, 2, 2, 2, rows // 2, LANES), BF16),
            pltpu.VMEM((in_pair, lines, 2 * LANES), BF16),
            pltpu.VMEM((in_pair, lines, 2 * LANES), BF16),
            pltpu.VMEM(orders.shape, jnp.int32),
            dma((5,)),
            pltpu.SemaphoreType.REGULAR((devices // 8 - 1,)),
            dma((2,)),
            dma((2,)),
            dma((2,)),
            dma((2, 2 * (devices // 8) + 1)),
            dma((1,)),
            dma((2, devices // 8)),
            dma((1,)),
            dma((1,)),
            dma((2,)),
            dma((2,)),
            dma((1,)),
            dma((1,)),
        ],
        compiler_params=pltpu.CompilerParams(
            collective_id=0, has_side_effects=True, vmem_limit_bytes=60 * 2**20
        ),
    )(branch, orders, gate_a, gate_b)


def local(branch_in, column_order, gate_a, gate_b):
    join_scale = (2.0 * SHARED) ** (-0.5)
    devices = lax.axis_size("mode")
    me = lax.axis_index("mode")
    branches, parts, rows, width = branch_in.shape
    quarter = SHARED // width
    holders = devices // (2 * quarter)
    share = rows // (quarter * holders)
    pair = me // (quarter * holders)
    lines = 2 * parts * share
    if lines == 2 * HIGH and holders == KEPT and devices == HIGH * KEPT == width // devices:
        done = run_whole(branch_in, column_order, gate_a, gate_b, devices)
        return done.reshape(2, lines, 2, LANES)
    dealt = branch_in.reshape(2, 2, parts, holders, share, quarter, width)
    dealt = dealt.transpose(0, 5, 3, 2, 1, 4, 6).reshape(devices, parts, 2, share, width)
    orders = lax.dynamic_slice_in_dim(column_order, 2 * pair, 2, 0)
    whole_a = lax.all_gather(gate_a, "mode", axis=1, tiled=True)
    whole_b = lax.all_gather(gate_b, "mode", axis=1, tiled=True)
    dealt = lax.all_to_all(dealt, "mode", split_axis=0, concat_axis=0, tiled=True)
    state = dealt.transpose(1, 0, 2, 3, 4)
    state = layers_plain(state, orders, whole_a, whole_b)

    split = holders // KEPT
    piece = width // split
    free = devices * rows * width // (SHARED * KEPT)
    own_group = [
        [start * holders + h for h in range(holders)] for start in range(2 * quarter)
    ]
    pair_group = [
        [start * quarter * holders + d for d in range(quarter * holders)] for start in range(2)
    ]
    left = state[:, :, 0].reshape(parts, KEPT, devices // KEPT, share, split, piece)
    left = left.transpose(1, 4, 0, 2, 3, 5).reshape(
        holders, parts, devices // KEPT, share, piece
    )
    left = lax.all_to_all(
        left, "mode", split_axis=0, concat_axis=0, tiled=True, axis_index_groups=own_group
    )
    left = left.transpose(1, 2, 0, 3, 4).reshape(parts, free, piece)
    right = state[:, :, 1].reshape(parts, quarter, split, devices // (quarter * split), share, width)
    line = rows * width
    step = KEPT * free
    if width % step == 0:
        several = width // step
        right = right.reshape(
            parts, quarter, split, devices // (quarter * split), share, several, KEPT, free
        )
        right = right.transpose(1, 6, 2, 0, 3, 4, 5, 7)
        right = right.reshape(
            quarter * KEPT * split, parts, devices // (quarter * split), share, several, free
        )
        right = lax.all_to_all(
            right, "mode", split_axis=0, concat_axis=0, tiled=True, axis_index_groups=pair_group
        )
        right = right.reshape(
            quarter, holders, parts, devices // (quarter * split), share, several, free
        )
        right = right.transpose(2, 3, 1, 4, 0, 5, 6).reshape(parts, piece, free)
    else:
        spans = step // width
        kept_row = KEPT // spans
        right = right.reshape(
            parts, quarter, split, devices // (quarter * split), share, kept_row, free
        )
        own_j = me // holders % quarter
        g_high = own_j % spans
        slots = jnp.zeros(
            (quarter, spans, kept_row, split, parts, devices // (quarter * split), share, free), BF16
        )
        filled = right.transpose(1, 5, 2, 0, 3, 4, 6)
        slots = lax.dynamic_update_slice_in_dim(slots, filled[:, None], g_high, 1)
        slots = slots.reshape(
            quarter * KEPT * split, parts, devices // (quarter * split), share, free
        )
        slots = lax.all_to_all(
            slots, "mode", split_axis=0, concat_axis=0, tiled=True, axis_index_groups=pair_group
        )
        slots = slots.reshape(
            quarter // spans, spans, holders, parts, devices // (quarter * split), share, free
        )
        my_g = me % holders // split
        slots = lax.dynamic_index_in_dim(slots, my_g // kept_row, 1, keepdims=False)
        right = slots.transpose(2, 3, 1, 4, 0, 5).reshape(parts, piece, free)
    real_part, imag_part = complex_dot(left[0], left[1], right[0], right[1])
    partial = jnp.stack([real_part, imag_part], axis=1)
    return finish(partial, join_scale, devices, quarter, split)


def finish(partial, join_scale, devices, quarter, split):
    me = lax.axis_index("mode")
    free = partial.shape[0]
    holders = devices // (2 * quarter)
    sum_group = [
        [((p * quarter + j) * KEPT + g) * split + w for j in range(quarter) for w in range(split)]
        for p in range(2)
        for g in range(KEPT)
    ]
    count = quarter * split
    chunks = partial.astype(BF16).reshape(count, free // count, 2, free)
    chunks = lax.all_to_all(
        chunks, "mode", split_axis=0, concat_axis=0, tiled=True, axis_index_groups=sum_group
    )
    done = (jnp.sum(chunks.astype(F32), axis=0) * join_scale).astype(BF16)
    halves = done.reshape(2, free // (2 * count), 2, free)
    pair = me // (quarter * holders)
    same = lax.dynamic_index_in_dim(halves, pair, 0, keepdims=False)
    other = lax.dynamic_index_in_dim(halves, 1 - pair, 0, keepdims=False)
    same_pairs, other_pairs = [], []
    for d in range(devices):
        p, j, g, w = (
            d // (quarter * holders),
            d // holders % quarter,
            d // split % KEPT,
            d % split,
        )
        base = g * (devices // KEPT) + 2 * (j * split + w)
        same_pairs.append((d, base + p))
        other_pairs.append((d, base + 1 - p))
    from_same = lax.ppermute(same, "mode", same_pairs)
    from_other = lax.ppermute(other, "mode", other_pairs)
    parity = me % 2
    first = jnp.where(parity == 0, from_same, from_other)
    second = jnp.where(parity == 0, from_other, from_same)
    return jnp.stack([first, second])


def solution(mesh):
    in_specs = (
        P(None, None, ("cuts", "mode"), None),
        P(),
        P(None, "mode", None),
        P(None, "mode", None),
    )
    out_specs = P(None, ("cuts", "mode"), None, None)
    return jax.shard_map(local, mesh=mesh, in_specs=in_specs, out_specs=out_specs, check_vma=False)
```
